512 devices in a mesh: line: 16 (over z), bus: 32 (over x, y, core).
Axes of the slice: x: 4, y: 4, z: 16, core: 2. Of those that a mesh axis runs over, the one named last changes fastest.
Arguments:
- transfer_factors: float32 [4096, 65536], P('line', 'bus'), may hold values from -0.24 to 0.24
- line_flows: float32 [4096], P('line'), may hold values from -6 to 6
- from_bus: int32 [4096], replicated, may hold values from 0 to 65535
- to_bus: int32 [4096], replicated, may hold values from 0 to 65535
- tripped: int32 [2, 64], replicated, may hold values from 0 to 4095, as said below
Outputs:
- new_factors: float32 [4096, 65536], P('line', 'bus')
- new_flows: float32 [4096], P('line')
The draws below stay inside these ranges and needn't reach their ends.
Inputs may be any that keep to these rules, and one draw needn't show every extreme that they name: No line is tripped twice; in every segment at most 8 tripped lines lie in one aligned block of 256 consecutive lines, and some block holds exactly 8.
All inputs are finite; a program needn't handle non-finite values.
Results may differ from the reference program's by a relative error of at most 0.00018.
Values sent between devices are 32-bit elements; how exact they have to be, the bound alone decides.
A program may use at most 64 MiB of HBM per device.

```python
import jax
import jax.numpy as jnp
from jax import lax

NB = 65536
K = 64
STEPS = 2
L_DEV = 256
LINES = 4096
CAP = 8
N_LINE = 16


def move_to(order, value, target_pos):
    found = jnp.argmax(order == value).astype(jnp.int32)
    displaced = order[target_pos]
    return order.at[found].set(displaced).at[target_pos].set(value)


def draw_tripped(key, part):
    half_blocks = N_LINE // 2
    segments = []
    for segment_index in range(STEPS):
        segment_key = jax.random.fold_in(jax.random.fold_in(key, 11), segment_index)
        block_order = jax.random.permutation(segment_key, N_LINE).astype(jnp.int32)
        forced_block = 0 if segment_index == 0 else N_LINE - 1
        block_order = move_to(block_order, jnp.int32(forced_block), 0)
        blocks = block_order[:half_blocks]

        def block_rows(block):
            row_key = jax.random.fold_in(jax.random.fold_in(key, 23), block)
            local_order = jax.random.permutation(row_key, L_DEV).astype(jnp.int32)
            is_first = block == 0
            is_last = block == N_LINE - 1
            target_row = jnp.where(is_first, 0, jnp.where(is_last, L_DEV - 1, local_order[0])).astype(jnp.int32)
            target_pos = jnp.where(is_last, CAP, 0).astype(jnp.int32)
            local_order = move_to(local_order, target_row, target_pos)
            return block * L_DEV + lax.dynamic_slice_in_dim(local_order, segment_index * CAP, CAP)
        chosen = jax.vmap(block_rows)(blocks).reshape(-1)
        segments.append(jax.random.permutation(jax.random.fold_in(segment_key, 5), chosen))
    return jnp.stack(segments).astype(jnp.int32)


def place_ends(values, rng, least, largest):
    longest = values.shape.index(max(values.shape))
    spots = []
    for shift in (0, 1):
        where = [jax.random.randint(jax.random.fold_in(rng, axis), (), 0, length) for axis, length in enumerate(values.shape)]
        where[longest] = (where[longest] + shift) % values.shape[longest]
        spots.append(tuple(where))
    return values.at[spots[0]].set(least).at[spots[1]].set(largest)


def level_of(key, extent, pieces, smallest, largest):
    gain, own = 1.0, jax.random.fold_in(key, 6)
    for position, parts in pieces:
        heights = jnp.exp(jax.random.uniform(jax.random.fold_in(own, position), (parts,), jnp.float32, smallest / len(pieces), largest / len(pieces)))
        gain = gain * jnp.repeat(heights, extent[position] // parts).reshape([-1 if axis == position else 1 for axis in range(len(extent))])
    return gain


def normal_values(own_key, shape, spread, bound, cuts=(), kind=jnp.bfloat16):
    result = jax.random.normal(own_key, shape, jnp.float32) * spread
    if len(cuts) > 0:
        result = level_of(own_key, shape, cuts, -0.22, 0.18) * result
    return jnp.clip(result, min=-bound, max=bound).astype(kind)


def setup_inputs(seed: int = 0) -> dict:
    key_of = jax.random.split(jax.random.key(seed), 6)
    transfer_factors = normal_values(key_of[0], (LINES, NB), 0.04, 0.24, ((0, 16), (1, 32)), jnp.float32)
    line_flows = normal_values(key_of[1], (LINES,), 1.0, 6.0, ((0, 16),), jnp.float32)
    from_bus = place_ends(jax.random.randint(key_of[2], (LINES,), 0, NB), jax.random.fold_in(key_of[2], 1), 0, NB - 1).astype(jnp.int32)
    to_bus = place_ends(jax.random.randint(key_of[3], (LINES,), 0, NB), jax.random.fold_in(key_of[3], 1), 0, NB - 1).astype(jnp.int32)
    tripped = draw_tripped(jax.random.fold_in(key_of[5], 71), 0)
    return {"transfer_factors": transfer_factors, "line_flows": line_flows, "from_bus": from_bus, "to_bus": to_bus, "tripped": tripped}


def chol_solve(factor_lower, right):
    middle = lax.linalg.triangular_solve(factor_lower, right, left_side=True, lower=True)
    return lax.linalg.triangular_solve(factor_lower, middle, left_side=True, lower=True, transpose_a=True)

def reference(transfer_factors, line_flows, from_bus, to_bus, tripped):
    precise = lax.Precision.HIGHEST
    factors = transfer_factors
    flows_now = line_flows
    for segment_index in range(STEPS):
        outage_ids = tripped[segment_index]
        terminal = jnp.take(factors, jnp.take(from_bus, outage_ids), axis=1) - jnp.take(factors, jnp.take(to_bus, outage_ids), axis=1)
        outage_rows = jnp.take(factors, outage_ids, axis=0)
        outage_flows = jnp.take(flows_now, outage_ids)
        capacitance = jnp.eye(K, dtype=jnp.float32) - jnp.take(terminal, outage_ids, axis=0)
        factor_lower = jnp.linalg.cholesky(jnp.dot(capacitance, capacitance.T, precision=precise))
        update_weights = chol_solve(factor_lower, jnp.dot(capacitance, terminal.T, precision=precise))
        factors = factors + jnp.dot(update_weights.T, outage_rows, precision=precise)
        flows_now = flows_now + jnp.dot(update_weights.T, outage_flows, precision=precise)
        keep_mask = jnp.ones((LINES,), jnp.float32).at[outage_ids].set(0.0)
        factors = factors * keep_mask[:, None]
        flows_now = flows_now * keep_mask
    return (factors, flows_now)
```

```python
import jax
import jax.numpy as jnp
from jax import lax
from jax.sharding import PartitionSpec as P

PRECISE = lax.Precision.HIGHEST


def chol_solve(factor_lower, right):
    middle = lax.linalg.triangular_solve(factor_lower, right, left_side=True, lower=True)
    return lax.linalg.triangular_solve(
        factor_lower, middle, left_side=True, lower=True, transpose_a=True
    )


def solve_weights(capacitance, terminal_rows):
    factor_lower = jnp.linalg.cholesky(jnp.dot(capacitance, capacitance.T, precision=PRECISE))
    return chol_solve(factor_lower, jnp.dot(capacitance, terminal_rows.T, precision=PRECISE))


def slot_layout(tripped, local_rows, cap):
    steps, outages = tripped.shape
    block = tripped // local_rows
    earlier = jnp.arange(outages)[None, :] < jnp.arange(outages)[:, None]
    same = (block[:, :, None] == block[:, None, :]) & earlier[None]
    rank = jnp.sum(same, axis=2).astype(jnp.int32)
    seg = jnp.arange(steps, dtype=jnp.int32)[:, None]
    slot = block * (steps * cap) + seg * cap + rank
    return block, rank, slot


def per_device(transfer_factors, line_flows, from_bus, to_bus, tripped):
    local_rows, local_cols = transfer_factors.shape
    steps, outages = tripped.shape
    cap = 8
    line_index = lax.axis_index("line")
    bus_index = lax.axis_index("bus")
    ids = tripped.reshape(-1)

    def local_column(bus):
        offset = bus - bus_index * local_cols
        inside = (offset >= 0) & (offset < local_cols)
        values = jnp.take(transfer_factors, jnp.clip(offset, 0, local_cols - 1), axis=1)
        return jnp.where(inside[None, :], values, 0.0)

    terminal_part = local_column(jnp.take(from_bus, ids)) - local_column(jnp.take(to_bus, ids))
    terminal = lax.psum(terminal_part, "bus")

    block, rank, slot = slot_layout(tripped, local_rows, cap)
    mine = (block == line_index)[:, None, :] & (
        rank[:, None, :] == jnp.arange(cap, dtype=jnp.int32)[None, :, None]
    )
    position = jnp.sum(jnp.where(mine, (tripped - line_index * local_rows)[:, None, :], 0), axis=2)
    valid = jnp.any(mine, axis=2).reshape(-1)
    position = position.reshape(-1)
    rows = jnp.where(valid[:, None], jnp.take(transfer_factors, position, axis=0), 0.0)
    small = jnp.concatenate(
        [jnp.take(terminal, position, axis=0), jnp.take(line_flows, position)[:, None]], axis=1
    )
    small = jnp.where(valid[:, None], small, 0.0)

    gathered_rows = lax.all_gather(rows, "line").reshape(-1, local_cols)
    gathered_small = lax.all_gather(small, "line").reshape(-1, small.shape[1])
    slot_flat = slot.reshape(-1)
    outage_rows = jnp.take(gathered_rows, slot_flat, axis=0)
    outage_small = jnp.take(gathered_small, slot_flat, axis=0)
    outage_terms = outage_small[:, : steps * outages]
    outage_flows = outage_small[:, steps * outages]

    identity = jnp.eye(outages, dtype=jnp.float32)
    row_global = line_index * local_rows + jnp.arange(local_rows, dtype=jnp.int32)
    hit = row_global[:, None] == tripped[0][None, :]
    keep1 = 1.0 - jnp.any(hit, axis=1).astype(jnp.float32)
    hit2 = row_global[:, None] == tripped[1][None, :]
    keep12 = keep1 * (1.0 - jnp.any(hit2, axis=1).astype(jnp.float32))

    s1 = slice(0, outages)
    s2 = slice(outages, 2 * outages)
    cap1 = identity - outage_terms[s1, s1]
    rhs1 = jnp.concatenate([terminal[:, s1], outage_terms[s2, s1]], axis=0)
    w1 = solve_weights(cap1, rhs1)
    w1t_local = w1[:, :local_rows].T
    w1t_out2 = w1[:, local_rows:].T
    terminal2 = keep1[:, None] * (
        terminal[:, s2] + jnp.dot(w1t_local, outage_terms[s1, s2], precision=PRECISE)
    )
    out2 = outage_terms[s2, s2] + jnp.dot(w1t_out2, outage_terms[s1, s2], precision=PRECISE)
    cap2 = identity - out2
    w2t = solve_weights(cap2, terminal2).T
    combined = jnp.concatenate(
        [w1t_local + jnp.dot(w2t, w1t_out2, precision=PRECISE), w2t], axis=1
    )

    factors = keep12[:, None] * (
        transfer_factors + jnp.dot(combined, outage_rows, precision=PRECISE)
    )
    flows = keep12 * (line_flows + jnp.dot(combined, outage_flows, precision=PRECISE))
    return (factors, flows)


def solution(mesh):
    placed = (P("line", "bus"), P("line"), P(), P(), P())
    return jax.shard_map(
        per_device,
        mesh=mesh,
        in_specs=placed,
        out_specs=(P("line", "bus"), P("line")),
        check_vma=False,
    )
```

```python
import functools

import jax
import jax.numpy as jnp
from jax import lax
from jax.experimental import pallas as pl
from jax.experimental.pallas import tpu as pltpu
from jax.sharding import PartitionSpec as P

PRECISE = lax.Precision.HIGHEST


def _mesh_id(axis, peer):
    coords = {"line": lax.axis_index("line"), "bus": lax.axis_index("bus")}
    coords[axis] = peer
    return (coords["line"], coords["bus"])


def _greet(axis, n):
    barrier = pltpu.get_barrier_semaphore()
    me = lax.axis_index(axis)

    def body(k, carry):
        peer = lax.rem(me + k, n)
        pl.semaphore_signal(
            barrier, 1, device_id=_mesh_id(axis, peer), device_id_type=pl.DeviceIdType.MESH
        )
        return carry

    lax.fori_loop(1, n, body, 0)
    pl.semaphore_wait(barrier, n - 1)


def _bus_reduce_kernel(n, x_ref, o_ref, recv, gathered, mine, s1, r1, s2, r2):
    me = lax.axis_index("bus")
    chunk = x_ref.shape[0] // n
    _greet("bus", n)

    def send1(k):
        peer = lax.rem(me + k, n)
        return pltpu.make_async_remote_copy(
            src_ref=x_ref.at[pl.ds(peer * chunk, chunk)],
            dst_ref=recv.at[k],
            send_sem=s1.at[k],
            recv_sem=r1.at[k],
            device_id=_mesh_id("bus", peer),
            device_id_type=pl.DeviceIdType.MESH,
        )

    def start1(k, carry):
        send1(k).start()
        return carry

    lax.fori_loop(1, n, start1, 0)
    total = x_ref[pl.ds(me * chunk, chunk), :]

    def finish1(k, acc):
        send1(k).wait()
        return acc + recv[k]

    total = lax.fori_loop(1, n, finish1, total)
    gathered[pl.ds(me * chunk, chunk), :] = total
    mine[...] = total

    def send2(k):
        peer = lax.rem(me + k, n)
        return pltpu.make_async_remote_copy(
            src_ref=mine,
            dst_ref=gathered.at[pl.ds(me * chunk, chunk)],
            send_sem=s2.at[k],
            recv_sem=r2.at[k],
            device_id=_mesh_id("bus", peer),
            device_id_type=pl.DeviceIdType.MESH,
        )

    def start2(k, carry):
        send2(k).start()
        return carry

    lax.fori_loop(1, n, start2, 0)

    def finish2(k, carry):
        send2(k).wait()
        return carry

    lax.fori_loop(1, n, finish2, 0)
    o_ref[...] = gathered[...]


def bus_reduce(x, n):
    rows, cols = x.shape
    chunk = rows // n
    vmem = pl.BlockSpec(memory_space=pltpu.VMEM)
    return pl.pallas_call(
        functools.partial(_bus_reduce_kernel, n),
        out_shape=jax.ShapeDtypeStruct((rows, cols), x.dtype),
        in_specs=[vmem],
        out_specs=vmem,
        scratch_shapes=[
            pltpu.VMEM((n, chunk, cols), x.dtype),
            pltpu.VMEM((rows, cols), x.dtype),
            pltpu.VMEM((chunk, cols), x.dtype),
            pltpu.SemaphoreType.DMA((n,)),
            pltpu.SemaphoreType.DMA((n,)),
            pltpu.SemaphoreType.DMA((n,)),
            pltpu.SemaphoreType.DMA((n,)),
        ],
        compiler_params=pltpu.CompilerParams(collective_id=0, has_side_effects=True),
    )(x)


def _line_gather_kernel(n, x_ref, o_ref, gathered, s1, r1):
    me = lax.axis_index("line")
    _greet("line", n)

    def send(k):
        peer = lax.rem(me + k, n)
        return pltpu.make_async_remote_copy(
            src_ref=x_ref,
            dst_ref=gathered.at[me],
            send_sem=s1.at[k],
            recv_sem=r1.at[k],
            device_id=_mesh_id("line", peer),
            device_id_type=pl.DeviceIdType.MESH,
        )

    def start(k, carry):
        send(k).start()
        return carry

    lax.fori_loop(1, n, start, 0)
    gathered[me] = x_ref[...]

    def finish(k, carry):
        send(k).wait()
        return carry

    lax.fori_loop(1, n, finish, 0)
    o_ref[...] = gathered[...]


def line_gather(x, n):
    vmem = pl.BlockSpec(memory_space=pltpu.VMEM)
    return pl.pallas_call(
        functools.partial(_line_gather_kernel, n),
        out_shape=jax.ShapeDtypeStruct((n,) + x.shape, x.dtype),
        in_specs=[vmem],
        out_specs=vmem,
        scratch_shapes=[
            pltpu.VMEM((n,) + x.shape, x.dtype),
            pltpu.SemaphoreType.DMA((n,)),
            pltpu.SemaphoreType.DMA((n,)),
        ],
        compiler_params=pltpu.CompilerParams(collective_id=1, has_side_effects=True),
    )(x)


def chol_solve(factor_lower, right):
    middle = lax.linalg.triangular_solve(factor_lower, right, left_side=True, lower=True)
    return lax.linalg.triangular_solve(
        factor_lower, middle, left_side=True, lower=True, transpose_a=True
    )


def solve_weights(capacitance, terminal_rows):
    factor_lower = jnp.linalg.cholesky(jnp.dot(capacitance, capacitance.T, precision=PRECISE))
    return chol_solve(factor_lower, jnp.dot(capacitance, terminal_rows.T, precision=PRECISE))


def slot_layout(tripped, local_rows, cap):
    steps, outages = tripped.shape
    block = tripped // local_rows
    earlier = jnp.arange(outages)[None, :] < jnp.arange(outages)[:, None]
    same = (block[:, :, None] == block[:, None, :]) & earlier[None]
    rank = jnp.sum(same, axis=2).astype(jnp.int32)
    seg = jnp.arange(steps, dtype=jnp.int32)[:, None]
    slot = block * (steps * cap) + seg * cap + rank
    return block, rank, slot


def per_device(transfer_factors, line_flows, from_bus, to_bus, tripped):
    local_rows, local_cols = transfer_factors.shape
    steps, outages = tripped.shape
    cap = 8
    line_index = lax.axis_index("line")
    bus_index = lax.axis_index("bus")
    ids = tripped.reshape(-1)

    def local_column(bus):
        offset = bus - bus_index * local_cols
        inside = (offset >= 0) & (offset < local_cols)
        values = jnp.take(transfer_factors, jnp.clip(offset, 0, local_cols - 1), axis=1)
        return jnp.where(inside[None, :], values, 0.0)

    terminal_part = local_column(jnp.take(from_bus, ids)) - local_column(jnp.take(to_bus, ids))
    terminal = bus_reduce(terminal_part, lax.axis_size("bus"))

    block, rank, slot = slot_layout(tripped, local_rows, cap)
    mine = (block == line_index)[:, None, :] & (
        rank[:, None, :] == jnp.arange(cap, dtype=jnp.int32)[None, :, None]
    )
    position = jnp.sum(jnp.where(mine, (tripped - line_index * local_rows)[:, None, :], 0), axis=2)
    valid = jnp.any(mine, axis=2).reshape(-1)
    position = position.reshape(-1)
    rows = jnp.where(valid[:, None], jnp.take(transfer_factors, position, axis=0), 0.0)
    small = jnp.concatenate(
        [
            jnp.take(terminal, position, axis=0),
            jnp.take(line_flows, position)[:, None],
            jnp.zeros((position.shape[0], 127), jnp.float32),
        ],
        axis=1,
    )
    small = jnp.where(valid[:, None], small, 0.0)

    gathered_rows = lax.all_gather(rows, "line").reshape(-1, local_cols)
    gathered_small = line_gather(small, lax.axis_size("line")).reshape(-1, small.shape[1])
    slot_flat = slot.reshape(-1)
    outage_rows = jnp.take(gathered_rows, slot_flat, axis=0)
    outage_small = jnp.take(gathered_small, slot_flat, axis=0)
    outage_terms = outage_small[:, : steps * outages]
    outage_flows = outage_small[:, steps * outages]

    identity = jnp.eye(outages, dtype=jnp.float32)
    row_global = line_index * local_rows + jnp.arange(local_rows, dtype=jnp.int32)
    hit = row_global[:, None] == tripped[0][None, :]
    keep1 = 1.0 - jnp.any(hit, axis=1).astype(jnp.float32)
    hit2 = row_global[:, None] == tripped[1][None, :]
    keep12 = keep1 * (1.0 - jnp.any(hit2, axis=1).astype(jnp.float32))

    s1 = slice(0, outages)
    s2 = slice(outages, 2 * outages)
    cap1 = identity - outage_terms[s1, s1]
    rhs1 = jnp.concatenate([terminal[:, s1], outage_terms[s2, s1]], axis=0)
    w1 = solve_weights(cap1, rhs1)
    w1t_local = w1[:, :local_rows].T
    w1t_out2 = w1[:, local_rows:].T
    terminal2 = keep1[:, None] * (
        terminal[:, s2] + jnp.dot(w1t_local, outage_terms[s1, s2], precision=PRECISE)
    )
    out2 = outage_terms[s2, s2] + jnp.dot(w1t_out2, outage_terms[s1, s2], precision=PRECISE)
    cap2 = identity - out2
    w2t = solve_weights(cap2, terminal2).T
    combined = jnp.concatenate(
        [w1t_local + jnp.dot(w2t, w1t_out2, precision=PRECISE), w2t], axis=1
    )

    factors = keep12[:, None] * (
        transfer_factors + jnp.dot(combined, outage_rows, precision=PRECISE)
    )
    flows = keep12 * (line_flows + jnp.dot(combined, outage_flows, precision=PRECISE))
    return (factors, flows)


def solution(mesh):
    placed = (P("line", "bus"), P("line"), P(), P(), P())
    return jax.shard_map(
        per_device,
        mesh=mesh,
        in_specs=placed,
        out_specs=(P("line", "bus"), P("line")),
        check_vma=False,
    )
```

```python
import functools

import jax
import jax.numpy as jnp
from jax import lax
from jax.experimental import pallas as pl
from jax.experimental.pallas import tpu as pltpu
from jax.sharding import PartitionSpec as P

PRECISE = lax.Precision.HIGHEST


def _mesh_id(axis, peer):
    coords = {"line": lax.axis_index("line"), "bus": lax.axis_index("bus")}
    coords[axis] = peer
    return (coords["line"], coords["bus"])


def _greet(axis, n):
    barrier = pltpu.get_barrier_semaphore()
    me = lax.axis_index(axis)

    def body(k, carry):
        peer = lax.rem(me + k, n)
        pl.semaphore_signal(
            barrier, 1, device_id=_mesh_id(axis, peer), device_id_type=pl.DeviceIdType.MESH
        )
        return carry

    lax.fori_loop(1, n, body, 0)
    pl.semaphore_wait(barrier, n - 1)


def _remote(src, dst, send_sem, recv_sem, axis, peer):
    return pltpu.make_async_remote_copy(
        src_ref=src,
        dst_ref=dst,
        send_sem=send_sem,
        recv_sem=recv_sem,
        device_id=_mesh_id(axis, peer),
        device_id_type=pl.DeviceIdType.MESH,
    )


def _exchange_kernel(
    n_bus, n_line, x_ref, rows_ref, o_ref, o_rows, recv, gathered, mine, held,
    s1, r1, s2, r2, sr, rr, sl, rl,
):
    me = lax.axis_index("bus")
    here = lax.axis_index("line")
    right = lax.rem(here + 1, n_line)
    left = lax.rem(here + n_line - 1, n_line)
    chunk = x_ref.shape[0] // n_bus
    to_right = n_line // 2
    to_left = n_line - 1 - to_right

    barrier = pltpu.get_barrier_semaphore()

    def greet(k, carry):
        pl.semaphore_signal(
            barrier, 1, device_id=_mesh_id("bus", lax.rem(me + k, n_bus)),
            device_id_type=pl.DeviceIdType.MESH,
        )
        return carry

    lax.fori_loop(1, n_bus, greet, 0)
    for neighbour in (left, right):
        pl.semaphore_signal(
            barrier, 1, device_id=_mesh_id("line", neighbour), device_id_type=pl.DeviceIdType.MESH
        )
    pl.semaphore_wait(barrier, n_bus - 1 + 2)

    def ring(step):
        copies = []
        if step <= to_right:
            origin = lax.rem(here - (step - 1) + n_line, n_line)
            src = rows_ref if step == 1 else held.at[origin]
            copies.append(_remote(src, held.at[origin], sr.at[step - 1], rr.at[step - 1], "line", right))
        if step <= to_left:
            origin = lax.rem(here + (step - 1), n_line)
            src = rows_ref if step == 1 else held.at[origin]
            copies.append(_remote(src, held.at[origin], sl.at[step - 1], rl.at[step - 1], "line", left))
        return copies

    first = ring(1)
    for copy in first:
        copy.start()

    def send1(k):
        peer = lax.rem(me + k, n_bus)
        return _remote(x_ref.at[pl.ds(peer * chunk, chunk)], recv.at[k], s1.at[k], r1.at[k], "bus", peer)

    def start1(k, carry):
        send1(k).start()
        return carry

    lax.fori_loop(1, n_bus, start1, 0)
    held[here] = rows_ref[...]
    total = x_ref[pl.ds(me * chunk, chunk), :]

    def finish1(k, acc):
        send1(k).wait()
        return acc + recv[k]

    total = lax.fori_loop(1, n_bus, finish1, total)
    gathered[pl.ds(me * chunk, chunk), :] = total
    mine[...] = total

    def send2(k):
        peer = lax.rem(me + k, n_bus)
        return _remote(mine, gathered.at[pl.ds(me * chunk, chunk)], s2.at[k], r2.at[k], "bus", peer)

    def start2(k, carry):
        send2(k).start()
        return carry

    lax.fori_loop(1, n_bus, start2, 0)

    for copy in first:
        copy.wait()
    for step in range(2, to_right + 1):
        copies = ring(step)
        for copy in copies:
            copy.start()
        for copy in copies:
            copy.wait()

    def finish2(k, carry):
        send2(k).wait()
        return carry

    lax.fori_loop(1, n_bus, finish2, 0)
    o_ref[...] = gathered[...]
    o_rows[...] = held[...]


def exchange(x, rows, n_bus, n_line):
    x_rows, x_cols = x.shape
    chunk = x_rows // n_bus
    vmem = pl.BlockSpec(memory_space=pltpu.VMEM)
    held_shape = (n_line,) + rows.shape
    return pl.pallas_call(
        functools.partial(_exchange_kernel, n_bus, n_line),
        out_shape=(
            jax.ShapeDtypeStruct(x.shape, x.dtype),
            jax.ShapeDtypeStruct(held_shape, rows.dtype),
        ),
        in_specs=[vmem, vmem],
        out_specs=(vmem, vmem),
        scratch_shapes=[
            pltpu.VMEM((n_bus, chunk, x_cols), x.dtype),
            pltpu.VMEM(x.shape, x.dtype),
            pltpu.VMEM((chunk, x_cols), x.dtype),
            pltpu.VMEM(held_shape, rows.dtype),
        ]
        + [pltpu.SemaphoreType.DMA((n_bus,))] * 4
        + [pltpu.SemaphoreType.DMA((n_line,))] * 4,
        compiler_params=pltpu.CompilerParams(
            collective_id=0, has_side_effects=True, vmem_limit_bytes=48 * 1024 * 1024
        ),
    )(x, rows)


def _line_gather_kernel(n, x_ref, o_ref, gathered, s1, r1):
    me = lax.axis_index("line")
    _greet("line", n)

    def send(k):
        peer = lax.rem(me + k, n)
        return pltpu.make_async_remote_copy(
            src_ref=x_ref,
            dst_ref=gathered.at[me],
            send_sem=s1.at[k],
            recv_sem=r1.at[k],
            device_id=_mesh_id("line", peer),
            device_id_type=pl.DeviceIdType.MESH,
        )

    def start(k, carry):
        send(k).start()
        return carry

    lax.fori_loop(1, n, start, 0)
    gathered[me] = x_ref[...]

    def finish(k, carry):
        send(k).wait()
        return carry

    lax.fori_loop(1, n, finish, 0)
    o_ref[...] = gathered[...]


def line_gather(x, n):
    vmem = pl.BlockSpec(memory_space=pltpu.VMEM)
    return pl.pallas_call(
        functools.partial(_line_gather_kernel, n),
        out_shape=jax.ShapeDtypeStruct((n,) + x.shape, x.dtype),
        in_specs=[vmem],
        out_specs=vmem,
        scratch_shapes=[
            pltpu.VMEM((n,) + x.shape, x.dtype),
            pltpu.SemaphoreType.DMA((n,)),
            pltpu.SemaphoreType.DMA((n,)),
        ],
        compiler_params=pltpu.CompilerParams(collective_id=1, has_side_effects=True),
    )(x)


def chol_solve(factor_lower, right):
    middle = lax.linalg.triangular_solve(factor_lower, right, left_side=True, lower=True)
    return lax.linalg.triangular_solve(
        factor_lower, middle, left_side=True, lower=True, transpose_a=True
    )


def solve_weights(capacitance, terminal_rows):
    factor_lower = jnp.linalg.cholesky(jnp.dot(capacitance, capacitance.T, precision=PRECISE))
    return chol_solve(factor_lower, jnp.dot(capacitance, terminal_rows.T, precision=PRECISE))


def slot_layout(tripped, local_rows, cap):
    steps, outages = tripped.shape
    block = tripped // local_rows
    earlier = jnp.arange(outages)[None, :] < jnp.arange(outages)[:, None]
    same = (block[:, :, None] == block[:, None, :]) & earlier[None]
    rank = jnp.sum(same, axis=2).astype(jnp.int32)
    seg = jnp.arange(steps, dtype=jnp.int32)[:, None]
    slot = block * (steps * cap) + seg * cap + rank
    return block, rank, slot


def per_device(transfer_factors, line_flows, from_bus, to_bus, tripped):
    local_rows, local_cols = transfer_factors.shape
    steps, outages = tripped.shape
    cap = 8
    line_index = lax.axis_index("line")
    bus_index = lax.axis_index("bus")
    ids = tripped.reshape(-1)

    def local_column(bus):
        offset = bus - bus_index * local_cols
        inside = (offset >= 0) & (offset < local_cols)
        values = jnp.take(transfer_factors, jnp.clip(offset, 0, local_cols - 1), axis=1)
        return jnp.where(inside[None, :], values, 0.0)

    terminal_part = local_column(jnp.take(from_bus, ids)) - local_column(jnp.take(to_bus, ids))

    block, rank, slot = slot_layout(tripped, local_rows, cap)
    mine = (block == line_index)[:, None, :] & (
        rank[:, None, :] == jnp.arange(cap, dtype=jnp.int32)[None, :, None]
    )
    position = jnp.sum(jnp.where(mine, (tripped - line_index * local_rows)[:, None, :], 0), axis=2)
    valid = jnp.any(mine, axis=2).reshape(-1)
    position = position.reshape(-1)
    rows = jnp.where(valid[:, None], jnp.take(transfer_factors, position, axis=0), 0.0)
    terminal, gathered_rows = exchange(
        terminal_part, rows, lax.axis_size("bus"), lax.axis_size("line")
    )
    gathered_rows = gathered_rows.reshape(-1, local_cols)
    small = jnp.concatenate(
        [
            jnp.take(terminal, position, axis=0),
            jnp.take(line_flows, position)[:, None],
            jnp.zeros((position.shape[0], 127), jnp.float32),
        ],
        axis=1,
    )
    small = jnp.where(valid[:, None], small, 0.0)

    gathered_small = line_gather(small, lax.axis_size("line")).reshape(-1, small.shape[1])
    slot_flat = slot.reshape(-1)
    outage_rows = jnp.take(gathered_rows, slot_flat, axis=0)
    outage_small = jnp.take(gathered_small, slot_flat, axis=0)
    outage_terms = outage_small[:, : steps * outages]
    outage_flows = outage_small[:, steps * outages]

    identity = jnp.eye(outages, dtype=jnp.float32)
    row_global = line_index * local_rows + jnp.arange(local_rows, dtype=jnp.int32)
    hit = row_global[:, None] == tripped[0][None, :]
    keep1 = 1.0 - jnp.any(hit, axis=1).astype(jnp.float32)
    hit2 = row_global[:, None] == tripped[1][None, :]
    keep12 = keep1 * (1.0 - jnp.any(hit2, axis=1).astype(jnp.float32))

    s1 = slice(0, outages)
    s2 = slice(outages, 2 * outages)
    cap1 = identity - outage_terms[s1, s1]
    rhs1 = jnp.concatenate([terminal[:, s1], outage_terms[s2, s1]], axis=0)
    w1 = solve_weights(cap1, rhs1)
    w1t_local = w1[:, :local_rows].T
    w1t_out2 = w1[:, local_rows:].T
    terminal2 = keep1[:, None] * (
        terminal[:, s2] + jnp.dot(w1t_local, outage_terms[s1, s2], precision=PRECISE)
    )
    out2 = outage_terms[s2, s2] + jnp.dot(w1t_out2, outage_terms[s1, s2], precision=PRECISE)
    cap2 = identity - out2
    w2t = solve_weights(cap2, terminal2).T
    combined = jnp.concatenate(
        [w1t_local + jnp.dot(w2t, w1t_out2, precision=PRECISE), w2t], axis=1
    )

    factors = keep12[:, None] * (
        transfer_factors + jnp.dot(combined, outage_rows, precision=PRECISE)
    )
    flows = keep12 * (line_flows + jnp.dot(combined, outage_flows, precision=PRECISE))
    return (factors, flows)


def solution(mesh):
    placed = (P("line", "bus"), P("line"), P(), P(), P())
    return jax.shard_map(
        per_device,
        mesh=mesh,
        in_specs=placed,
        out_specs=(P("line", "bus"), P("line")),
        check_vma=False,
    )
```

```python
import functools

import jax
import jax.numpy as jnp
from jax import lax
from jax.experimental import pallas as pl
from jax.experimental.pallas import tpu as pltpu
from jax.sharding import PartitionSpec as P

PRECISE = lax.Precision.HIGHEST


def _mesh_id(axis, peer):
    coords = {"line": lax.axis_index("line"), "bus": lax.axis_index("bus")}
    coords[axis] = peer
    return (coords["line"], coords["bus"])


def _greet(axis, n):
    barrier = pltpu.get_barrier_semaphore()
    me = lax.axis_index(axis)

    def body(k, carry):
        peer = lax.rem(me + k, n)
        pl.semaphore_signal(
            barrier, 1, device_id=_mesh_id(axis, peer), device_id_type=pl.DeviceIdType.MESH
        )
        return carry

    lax.fori_loop(1, n, body, 0)
    pl.semaphore_wait(barrier, n - 1)


def _remote(src, dst, send_sem, recv_sem, axis, peer):
    return pltpu.make_async_remote_copy(
        src_ref=src,
        dst_ref=dst,
        send_sem=send_sem,
        recv_sem=recv_sem,
        device_id=_mesh_id(axis, peer),
        device_id_type=pl.DeviceIdType.MESH,
    )


def _exchange_kernel(
    n_bus, n_line, pieces, pick_ref, x_ref, rows_ref, o_ref, o_rows, o_small,
    recv, gathered, mine, held, picked, got, s1, r1, s2, r2, sr, rr, sl, rl, s3, r3,
):
    me = lax.axis_index("bus")
    here = lax.axis_index("line")
    right = lax.rem(here + 1, n_line)
    left = lax.rem(here + n_line - 1, n_line)
    chunk = x_ref.shape[0] // n_bus
    piece = rows_ref.shape[0] // pieces
    to_right = n_line // 2
    to_left = n_line - 1 - to_right
    mesh_type = pl.DeviceIdType.MESH

    barrier = pltpu.get_barrier_semaphore()

    def greet_bus(k, carry):
        pl.semaphore_signal(
            barrier, 1, device_id=_mesh_id("bus", lax.rem(me + k, n_bus)), device_id_type=mesh_type
        )
        return carry

    def greet_line(k, carry):
        pl.semaphore_signal(
            barrier, 1, device_id=_mesh_id("line", lax.rem(here + k, n_line)),
            device_id_type=mesh_type,
        )
        return carry

    lax.fori_loop(1, n_bus, greet_bus, 0)
    lax.fori_loop(1, n_line, greet_line, 0)
    pl.semaphore_wait(barrier, n_bus - 1 + n_line - 1)

    def ring(step, part, toward):
        if toward == "right":
            origin = lax.rem(here - (step - 1) + n_line, n_line)
            peer, send_sem, recv_sem = right, sr, rr
        else:
            origin = lax.rem(here + (step - 1), n_line)
            peer, send_sem, recv_sem = left, sl, rl
        rows = pl.ds(part * piece, piece)
        src = rows_ref.at[rows] if step == 1 else held.at[origin, rows]
        slot = (step - 1) * pieces + part
        return _remote(src, held.at[origin, rows], send_sem.at[slot], recv_sem.at[slot], "line", peer)

    def ring_steps(toward):
        return to_right if toward == "right" else to_left

    for part in range(pieces):
        for toward in ("right", "left"):
            if ring_steps(toward) >= 1:
                ring(1, part, toward).start()

    def send1(k):
        peer = lax.rem(me + k, n_bus)
        return _remote(x_ref.at[pl.ds(peer * chunk, chunk)], recv.at[k], s1.at[k], r1.at[k], "bus", peer)

    def start1(k, carry):
        send1(k).start()
        return carry

    lax.fori_loop(1, n_bus, start1, 0)
    held[here] = rows_ref[...]
    total = x_ref[pl.ds(me * chunk, chunk), :]

    def finish1(k, acc):
        send1(k).wait()
        return acc + recv[k]

    total = lax.fori_loop(1, n_bus, finish1, total)
    gathered[pl.ds(me * chunk, chunk), :] = total
    mine[...] = total

    def send2(k):
        peer = lax.rem(me + k, n_bus)
        return _remote(mine, gathered.at[pl.ds(me * chunk, chunk)], s2.at[k], r2.at[k], "bus", peer)

    def start2(k, carry):
        send2(k).start()
        return carry

    lax.fori_loop(1, n_bus, start2, 0)

    for step in range(2, to_right + 1):
        for part in range(pieces):
            for toward in ("right", "left"):
                if step <= ring_steps(toward):
                    ring(step - 1, part, toward).wait_recv()
                    ring(step, part, toward).start()

    def finish2(k, carry):
        send2(k).wait()
        return carry

    lax.fori_loop(1, n_bus, finish2, 0)

    for i in range(picked.shape[0]):
        picked[pl.ds(i, 1), :] = gathered[pl.ds(pick_ref[i], 1), :]
    got[here] = picked[...]

    def send3(k):
        peer = lax.rem(here + k, n_line)
        return _remote(picked, got.at[here], s3.at[k], r3.at[k], "line", peer)

    def start3(k, carry):
        send3(k).start()
        return carry

    lax.fori_loop(1, n_line, start3, 0)

    for toward in ("right", "left"):
        last = ring_steps(toward)
        for part in range(pieces):
            if last >= 1:
                ring(last, part, toward).wait_recv()
        for step in range(1, last + 1):
            for part in range(pieces):
                ring(step, part, toward).wait_send()

    def finish3(k, carry):
        send3(k).wait()
        return carry

    lax.fori_loop(1, n_line, finish3, 0)
    o_ref[...] = gathered[...]
    o_rows[...] = held[...]
    o_small[...] = got[...]


def exchange(pick, x, rows, n_bus, n_line, pieces=2):
    x_rows, x_cols = x.shape
    chunk = x_rows // n_bus
    vmem = pl.BlockSpec(memory_space=pltpu.VMEM)
    smem = pl.BlockSpec(memory_space=pltpu.SMEM)
    held_shape = (n_line,) + rows.shape
    got_shape = (n_line, pick.shape[0], x_cols)
    return pl.pallas_call(
        functools.partial(_exchange_kernel, n_bus, n_line, pieces),
        out_shape=(
            jax.ShapeDtypeStruct(x.shape, x.dtype),
            jax.ShapeDtypeStruct(held_shape, rows.dtype),
            jax.ShapeDtypeStruct(got_shape, x.dtype),
        ),
        in_specs=[smem, vmem, vmem],
        out_specs=(vmem, vmem, vmem),
        scratch_shapes=[
            pltpu.VMEM((n_bus, chunk, x_cols), x.dtype),
            pltpu.VMEM(x.shape, x.dtype),
            pltpu.VMEM((chunk, x_cols), x.dtype),
            pltpu.VMEM(held_shape, rows.dtype),
            pltpu.VMEM((pick.shape[0], x_cols), x.dtype),
            pltpu.VMEM(got_shape, x.dtype),
        ]
        + [pltpu.SemaphoreType.DMA((n_bus,))] * 4
        + [pltpu.SemaphoreType.DMA((n_line * pieces,))] * 4
        + [pltpu.SemaphoreType.DMA((n_line,))] * 2,
        compiler_params=pltpu.CompilerParams(
            collective_id=0, has_side_effects=True, vmem_limit_bytes=48 * 1024 * 1024
        ),
    )(pick, x, rows)


def chol_solve(factor_lower, right):
    middle = lax.linalg.triangular_solve(factor_lower, right, left_side=True, lower=True)
    return lax.linalg.triangular_solve(
        factor_lower, middle, left_side=True, lower=True, transpose_a=True
    )


def solve_weights(capacitance, terminal_rows):
    factor_lower = jnp.linalg.cholesky(jnp.dot(capacitance, capacitance.T, precision=PRECISE))
    return chol_solve(factor_lower, jnp.dot(capacitance, terminal_rows.T, precision=PRECISE))


def slot_layout(tripped, local_rows, cap):
    steps, outages = tripped.shape
    block = tripped // local_rows
    earlier = jnp.arange(outages)[None, :] < jnp.arange(outages)[:, None]
    same = (block[:, :, None] == block[:, None, :]) & earlier[None]
    rank = jnp.sum(same, axis=2).astype(jnp.int32)
    seg = jnp.arange(steps, dtype=jnp.int32)[:, None]
    slot = block * (steps * cap) + seg * cap + rank
    return block, rank, slot


def per_device(transfer_factors, line_flows, from_bus, to_bus, tripped):
    local_rows, local_cols = transfer_factors.shape
    steps, outages = tripped.shape
    cap = 8
    line_index = lax.axis_index("line")
    bus_index = lax.axis_index("bus")
    ids = tripped.reshape(-1)

    def local_column(bus):
        offset = bus - bus_index * local_cols
        inside = (offset >= 0) & (offset < local_cols)
        values = jnp.take(transfer_factors, jnp.clip(offset, 0, local_cols - 1), axis=1)
        return jnp.where(inside[None, :], values, 0.0)

    terminal_part = local_column(jnp.take(from_bus, ids)) - local_column(jnp.take(to_bus, ids))

    block, rank, slot = slot_layout(tripped, local_rows, cap)
    mine = (block == line_index)[:, None, :] & (
        rank[:, None, :] == jnp.arange(cap, dtype=jnp.int32)[None, :, None]
    )
    position = jnp.sum(jnp.where(mine, (tripped - line_index * local_rows)[:, None, :], 0), axis=2)
    valid = jnp.any(mine, axis=2).reshape(-1)
    position = position.reshape(-1)
    rows = jnp.take(transfer_factors, position, axis=0)
    flows = jnp.take(line_flows, position)
    extra = jnp.zeros((position.shape[0], 128), jnp.float32).at[:, 0].set(flows)
    rows = jnp.where(valid[:, None], jnp.concatenate([rows, extra], axis=1), 0.0)
    pick = jnp.where(valid, position, 0).astype(jnp.int32)
    terminal, gathered_rows, gathered_small = exchange(
        pick, terminal_part, rows, lax.axis_size("bus"), lax.axis_size("line")
    )
    gathered_rows = gathered_rows.reshape(-1, rows.shape[1])
    gathered_small = gathered_small.reshape(-1, terminal.shape[1])
    slot_flat = slot.reshape(-1)
    outage_all = jnp.take(gathered_rows, slot_flat, axis=0)
    outage_rows = outage_all[:, :local_cols]
    outage_flows = outage_all[:, local_cols]
    outage_terms = jnp.take(gathered_small, slot_flat, axis=0)

    identity = jnp.eye(outages, dtype=jnp.float32)
    row_global = line_index * local_rows + jnp.arange(local_rows, dtype=jnp.int32)
    hit = row_global[:, None] == tripped[0][None, :]
    keep1 = 1.0 - jnp.any(hit, axis=1).astype(jnp.float32)
    hit2 = row_global[:, None] == tripped[1][None, :]
    keep12 = keep1 * (1.0 - jnp.any(hit2, axis=1).astype(jnp.float32))

    s1 = slice(0, outages)
    s2 = slice(outages, 2 * outages)
    cap1 = identity - outage_terms[s1, s1]
    rhs1 = jnp.concatenate([terminal[:, s1], outage_terms[s2, s1]], axis=0)
    w1 = solve_weights(cap1, rhs1)
    w1t_local = w1[:, :local_rows].T
    w1t_out2 = w1[:, local_rows:].T
    terminal2 = keep1[:, None] * (
        terminal[:, s2] + jnp.dot(w1t_local, outage_terms[s1, s2], precision=PRECISE)
    )
    out2 = outage_terms[s2, s2] + jnp.dot(w1t_out2, outage_terms[s1, s2], precision=PRECISE)
    cap2 = identity - out2
    w2t = solve_weights(cap2, terminal2).T
    combined = jnp.concatenate(
        [w1t_local + jnp.dot(w2t, w1t_out2, precision=PRECISE), w2t], axis=1
    )

    factors = keep12[:, None] * (
        transfer_factors + jnp.dot(combined, outage_rows, precision=PRECISE)
    )
    flows = keep12 * (line_flows + jnp.dot(combined, outage_flows, precision=PRECISE))
    return (factors, flows)


def solution(mesh):
    placed = (P("line", "bus"), P("line"), P(), P(), P())
    return jax.shard_map(
        per_device,
        mesh=mesh,
        in_specs=placed,
        out_specs=(P("line", "bus"), P("line")),
        check_vma=False,
    )
```

```python
import functools

import jax
import jax.numpy as jnp
from jax import lax
from jax.experimental import pallas as pl
from jax.experimental.pallas import tpu as pltpu
from jax.sharding import PartitionSpec as P

PRECISE = lax.Precision.HIGHEST


def _mesh_id(axis, peer):
    coords = {"line": lax.axis_index("line"), "bus": lax.axis_index("bus")}
    coords[axis] = peer
    return (coords["line"], coords["bus"])


def _greet(axis, n):
    barrier = pltpu.get_barrier_semaphore()
    me = lax.axis_index(axis)

    def body(k, carry):
        peer = lax.rem(me + k, n)
        pl.semaphore_signal(
            barrier, 1, device_id=_mesh_id(axis, peer), device_id_type=pl.DeviceIdType.MESH
        )
        return carry

    lax.fori_loop(1, n, body, 0)
    pl.semaphore_wait(barrier, n - 1)


def _remote(src, dst, send_sem, recv_sem, axis, peer):
    return pltpu.make_async_remote_copy(
        src_ref=src,
        dst_ref=dst,
        send_sem=send_sem,
        recv_sem=recv_sem,
        device_id=_mesh_id(axis, peer),
        device_id_type=pl.DeviceIdType.MESH,
    )


def _exchange_kernel(
    n_bus, n_line, pieces, pick_ref, x_ref, rows_ref, o_ref, o_rows, o_small,
    recv, gathered, mine, held, picked, got, s1, r1, s2, r2, sr, rr, sl, rl, tsr, trr, tsl, trl,
):
    me = lax.axis_index("bus")
    here = lax.axis_index("line")
    right = lax.rem(here + 1, n_line)
    left = lax.rem(here + n_line - 1, n_line)
    chunk = x_ref.shape[0] // n_bus
    piece = rows_ref.shape[0] // pieces
    to_right = n_line // 2
    to_left = n_line - 1 - to_right
    mesh_type = pl.DeviceIdType.MESH

    barrier = pltpu.get_barrier_semaphore()

    def greet_bus(k, carry):
        pl.semaphore_signal(
            barrier, 1, device_id=_mesh_id("bus", lax.rem(me + k, n_bus)), device_id_type=mesh_type
        )
        return carry

    lax.fori_loop(1, n_bus, greet_bus, 0)
    for neighbour in (left, right):
        pl.semaphore_signal(
            barrier, 1, device_id=_mesh_id("line", neighbour), device_id_type=mesh_type
        )
    pl.semaphore_wait(barrier, n_bus - 1 + 2)

    def ring_steps(toward):
        return to_right if toward == "right" else to_left

    def ring_copy(step, part, toward, first, buf, parts, sems):
        send_right, recv_right, send_left, recv_left = sems
        if toward == "right":
            origin = lax.rem(here - (step - 1) + n_line, n_line)
            peer, send_sem, recv_sem = right, send_right, recv_right
        else:
            origin = lax.rem(here + (step - 1), n_line)
            peer, send_sem, recv_sem = left, send_left, recv_left
        size = first.shape[0] // parts
        rows = pl.ds(part * size, size)
        src = first.at[rows] if step == 1 else buf.at[origin, rows]
        slot = (step - 1) * parts + part
        return _remote(src, buf.at[origin, rows], send_sem.at[slot], recv_sem.at[slot], "line", peer)

    def big(step):
        return lambda part, toward: ring_copy(step, part, toward, rows_ref, held, pieces, (sr, rr, sl, rl))

    def small(step):
        return lambda part, toward: ring_copy(step, part, toward, picked, got, 1, (tsr, trr, tsl, trl))

    def advance(copies, step, parts):
        for part in range(parts):
            for toward in ("right", "left"):
                if step <= ring_steps(toward):
                    if step > 1:
                        copies(step - 1)(part, toward).wait_recv()
                    copies(step)(part, toward).start()

    def drain(copies, parts):
        for toward in ("right", "left"):
            last = ring_steps(toward)
            for part in range(parts):
                if last >= 1:
                    copies(last)(part, toward).wait_recv()
            for step in range(1, last + 1):
                for part in range(parts):
                    copies(step)(part, toward).wait_send()

    advance(big, 1, pieces)

    def send1(k):
        peer = lax.rem(me + k, n_bus)
        return _remote(x_ref.at[pl.ds(peer * chunk, chunk)], recv.at[k], s1.at[k], r1.at[k], "bus", peer)

    def start1(k, carry):
        send1(k).start()
        return carry

    lax.fori_loop(1, n_bus, start1, 0)
    held[here] = rows_ref[...]
    advance(big, 2, pieces)
    total = x_ref[pl.ds(me * chunk, chunk), :]

    def finish1(k, acc):
        send1(k).wait()
        return acc + recv[k]

    total = lax.fori_loop(1, n_bus, finish1, total)
    gathered[pl.ds(me * chunk, chunk), :] = total
    mine[...] = total

    def send2(k):
        peer = lax.rem(me + k, n_bus)
        return _remote(mine, gathered.at[pl.ds(me * chunk, chunk)], s2.at[k], r2.at[k], "bus", peer)

    def start2(k, carry):
        send2(k).start()
        return carry

    lax.fori_loop(1, n_bus, start2, 0)
    advance(big, 3, pieces)

    def finish2(k, carry):
        send2(k).wait()
        return carry

    lax.fori_loop(1, n_bus, finish2, 0)

    for i in range(picked.shape[0]):
        picked[pl.ds(i, 1), :] = gathered[pl.ds(pick_ref[i], 1), :]
    got[here] = picked[...]
    advance(small, 1, 1)
    next_small = 2
    for step in range(4, to_right + 1):
        advance(big, step, pieces)
        advance(small, next_small, 1)
        next_small += 1
    for step in range(next_small, to_right + 1):
        advance(small, step, 1)
    drain(big, pieces)
    drain(small, 1)
    o_ref[...] = gathered[...]
    o_rows[...] = held[...]
    o_small[...] = got[...]


def exchange(pick, x, rows, n_bus, n_line, pieces=2):
    x_rows, x_cols = x.shape
    chunk = x_rows // n_bus
    vmem = pl.BlockSpec(memory_space=pltpu.VMEM)
    smem = pl.BlockSpec(memory_space=pltpu.SMEM)
    held_shape = (n_line,) + rows.shape
    got_shape = (n_line, pick.shape[0], x_cols)
    return pl.pallas_call(
        functools.partial(_exchange_kernel, n_bus, n_line, pieces),
        out_shape=(
            jax.ShapeDtypeStruct(x.shape, x.dtype),
            jax.ShapeDtypeStruct(held_shape, rows.dtype),
            jax.ShapeDtypeStruct(got_shape, x.dtype),
        ),
        in_specs=[smem, vmem, vmem],
        out_specs=(vmem, vmem, vmem),
        scratch_shapes=[
            pltpu.VMEM((n_bus, chunk, x_cols), x.dtype),
            pltpu.VMEM(x.shape, x.dtype),
            pltpu.VMEM((chunk, x_cols), x.dtype),
            pltpu.VMEM(held_shape, rows.dtype),
            pltpu.VMEM((pick.shape[0], x_cols), x.dtype),
            pltpu.VMEM(got_shape, x.dtype),
        ]
        + [pltpu.SemaphoreType.DMA((n_bus,))] * 4
        + [pltpu.SemaphoreType.DMA((n_line * pieces,))] * 4
        + [pltpu.SemaphoreType.DMA((n_line,))] * 4,
        compiler_params=pltpu.CompilerParams(
            collective_id=0, has_side_effects=True, vmem_limit_bytes=48 * 1024 * 1024
        ),
    )(pick, x, rows)


def chol_solve(factor_lower, right):
    middle = lax.linalg.triangular_solve(factor_lower, right, left_side=True, lower=True)
    return lax.linalg.triangular_solve(
        factor_lower, middle, left_side=True, lower=True, transpose_a=True
    )


def solve_weights(capacitance, terminal_rows):
    factor_lower = jnp.linalg.cholesky(jnp.dot(capacitance, capacitance.T, precision=PRECISE))
    return chol_solve(factor_lower, jnp.dot(capacitance, terminal_rows.T, precision=PRECISE))


def slot_layout(tripped, local_rows, cap):
    steps, outages = tripped.shape
    block = tripped // local_rows
    earlier = jnp.arange(outages)[None, :] < jnp.arange(outages)[:, None]
    same = (block[:, :, None] == block[:, None, :]) & earlier[None]
    rank = jnp.sum(same, axis=2).astype(jnp.int32)
    seg = jnp.arange(steps, dtype=jnp.int32)[:, None]
    slot = block * (steps * cap) + seg * cap + rank
    return block, rank, slot


def per_device(transfer_factors, line_flows, from_bus, to_bus, tripped):
    local_rows, local_cols = transfer_factors.shape
    steps, outages = tripped.shape
    cap = 8
    line_index = lax.axis_index("line")
    bus_index = lax.axis_index("bus")
    ids = tripped.reshape(-1)

    def local_column(bus):
        offset = bus - bus_index * local_cols
        inside = (offset >= 0) & (offset < local_cols)
        values = jnp.take(transfer_factors, jnp.clip(offset, 0, local_cols - 1), axis=1)
        return jnp.where(inside[None, :], values, 0.0)

    terminal_part = local_column(jnp.take(from_bus, ids)) - local_column(jnp.take(to_bus, ids))

    block, rank, slot = slot_layout(tripped, local_rows, cap)
    mine = (block == line_index)[:, None, :] & (
        rank[:, None, :] == jnp.arange(cap, dtype=jnp.int32)[None, :, None]
    )
    position = jnp.sum(jnp.where(mine, (tripped - line_index * local_rows)[:, None, :], 0), axis=2)
    valid = jnp.any(mine, axis=2).reshape(-1)
    position = position.reshape(-1)
    rows = jnp.take(transfer_factors, position, axis=0)
    flows = jnp.take(line_flows, position)
    extra = jnp.zeros((position.shape[0], 128), jnp.float32).at[:, 0].set(flows)
    rows = jnp.where(valid[:, None], jnp.concatenate([rows, extra], axis=1), 0.0)
    pick = jnp.where(valid, position, 0).astype(jnp.int32)
    terminal, gathered_rows, gathered_small = exchange(
        pick, terminal_part, rows, lax.axis_size("bus"), lax.axis_size("line")
    )
    gathered_rows = gathered_rows.reshape(-1, rows.shape[1])
    gathered_small = gathered_small.reshape(-1, terminal.shape[1])
    slot_flat = slot.reshape(-1)
    outage_all = jnp.take(gathered_rows, slot_flat, axis=0)
    outage_rows = outage_all[:, :local_cols]
    outage_flows = outage_all[:, local_cols]
    outage_terms = jnp.take(gathered_small, slot_flat, axis=0)

    identity = jnp.eye(outages, dtype=jnp.float32)
    row_global = line_index * local_rows + jnp.arange(local_rows, dtype=jnp.int32)
    hit = row_global[:, None] == tripped[0][None, :]
    keep1 = 1.0 - jnp.any(hit, axis=1).astype(jnp.float32)
    hit2 = row_global[:, None] == tripped[1][None, :]
    keep12 = keep1 * (1.0 - jnp.any(hit2, axis=1).astype(jnp.float32))

    s1 = slice(0, outages)
    s2 = slice(outages, 2 * outages)
    cap1 = identity - outage_terms[s1, s1]
    rhs1 = jnp.concatenate([terminal[:, s1], outage_terms[s2, s1]], axis=0)
    w1 = solve_weights(cap1, rhs1)
    w1t_local = w1[:, :local_rows].T
    w1t_out2 = w1[:, local_rows:].T
    terminal2 = keep1[:, None] * (
        terminal[:, s2] + jnp.dot(w1t_local, outage_terms[s1, s2], precision=PRECISE)
    )
    out2 = outage_terms[s2, s2] + jnp.dot(w1t_out2, outage_terms[s1, s2], precision=PRECISE)
    cap2 = identity - out2
    w2t = solve_weights(cap2, terminal2).T
    combined = jnp.concatenate(
        [w1t_local + jnp.dot(w2t, w1t_out2, precision=PRECISE), w2t], axis=1
    )

    factors = keep12[:, None] * (
        transfer_factors + jnp.dot(combined, outage_rows, precision=PRECISE)
    )
    flows = keep12 * (line_flows + jnp.dot(combined, outage_flows, precision=PRECISE))
    return (factors, flows)


def solution(mesh):
    placed = (P("line", "bus"), P("line"), P(), P(), P())
    return jax.shard_map(
        per_device,
        mesh=mesh,
        in_specs=placed,
        out_specs=(P("line", "bus"), P("line")),
        check_vma=False,
    )
```

```python
import functools

import jax
import jax.numpy as jnp
from jax import lax
from jax.experimental import pallas as pl
from jax.experimental.pallas import tpu as pltpu
from jax.sharding import PartitionSpec as P

PRECISE = lax.Precision.HIGHEST


def _mesh_id(axis, peer):
    coords = {"line": lax.axis_index("line"), "bus": lax.axis_index("bus")}
    coords[axis] = peer
    return (coords["line"], coords["bus"])


def _greet(axis, n):
    barrier = pltpu.get_barrier_semaphore()
    me = lax.axis_index(axis)

    def body(k, carry):
        peer = lax.rem(me + k, n)
        pl.semaphore_signal(
            barrier, 1, device_id=_mesh_id(axis, peer), device_id_type=pl.DeviceIdType.MESH
        )
        return carry

    lax.fori_loop(1, n, body, 0)
    pl.semaphore_wait(barrier, n - 1)


def _remote(src, dst, send_sem, recv_sem, axis, peer):
    return pltpu.make_async_remote_copy(
        src_ref=src,
        dst_ref=dst,
        send_sem=send_sem,
        recv_sem=recv_sem,
        device_id=_mesh_id(axis, peer),
        device_id_type=pl.DeviceIdType.MESH,
    )


def _exchange_kernel(
    n_bus, n_line, pieces, pick_ref, p_ref, ends_ref, rows_ref, o_ref, o_rows, o_small,
    x_ref, recv, gathered, mine, held, picked, got, s1, r1, s2, r2, sr, rr, sl, rl,
    tsr, trr, tsl, trl,
):
    me = lax.axis_index("bus")
    here = lax.axis_index("line")
    right = lax.rem(here + 1, n_line)
    left = lax.rem(here + n_line - 1, n_line)
    chunk = x_ref.shape[0] // n_bus
    piece = rows_ref.shape[0] // pieces
    to_right = n_line // 2
    to_left = n_line - 1 - to_right
    mesh_type = pl.DeviceIdType.MESH

    barrier = pltpu.get_barrier_semaphore()

    def greet_bus(k, carry):
        pl.semaphore_signal(
            barrier, 1, device_id=_mesh_id("bus", lax.rem(me + k, n_bus)), device_id_type=mesh_type
        )
        return carry

    lax.fori_loop(1, n_bus, greet_bus, 0)
    for neighbour in (left, right):
        pl.semaphore_signal(
            barrier, 1, device_id=_mesh_id("line", neighbour), device_id_type=mesh_type
        )
    pl.semaphore_wait(barrier, n_bus - 1 + 2)

    def ring_steps(toward):
        return to_right if toward == "right" else to_left

    def ring_copy(step, part, toward, first, buf, parts, sems):
        send_right, recv_right, send_left, recv_left = sems
        if toward == "right":
            origin = lax.rem(here - (step - 1) + n_line, n_line)
            peer, send_sem, recv_sem = right, send_right, recv_right
        else:
            origin = lax.rem(here + (step - 1), n_line)
            peer, send_sem, recv_sem = left, send_left, recv_left
        size = first.shape[0] // parts
        rows = pl.ds(part * size, size)
        src = first.at[rows] if step == 1 else buf.at[origin, rows]
        slot = (step - 1) * parts + part
        return _remote(src, buf.at[origin, rows], send_sem.at[slot], recv_sem.at[slot], "line", peer)

    def big(step):
        return lambda part, toward: ring_copy(step, part, toward, rows_ref, held, pieces, (sr, rr, sl, rl))

    def small(step):
        return lambda part, toward: ring_copy(step, part, toward, picked, got, 1, (tsr, trr, tsl, trl))

    def advance(copies, step, parts):
        for part in range(parts):
            for toward in ("right", "left"):
                if step <= ring_steps(toward):
                    if step > 1:
                        copies(step - 1)(part, toward).wait_recv()
                    copies(step)(part, toward).start()

    def drain(copies, parts):
        for toward in ("right", "left"):
            last = ring_steps(toward)
            for part in range(parts):
                if last >= 1:
                    copies(last)(part, toward).wait_recv()
            for step in range(1, last + 1):
                for part in range(parts):
                    copies(step)(part, toward).wait_send()

    advance(big, 1, pieces)

    local_cols = p_ref.shape[1]
    column = lax.broadcasted_iota(jnp.int32, (local_cols, ends_ref.shape[1]), 0)
    select = (column == ends_ref[0:1, :]).astype(jnp.float32) - (
        column == ends_ref[1:2, :]
    ).astype(jnp.float32)
    x_ref[...] = jnp.dot(
        p_ref[...], select, precision=PRECISE, preferred_element_type=jnp.float32
    )

    def send1(k):
        peer = lax.rem(me + k, n_bus)
        return _remote(x_ref.at[pl.ds(peer * chunk, chunk)], recv.at[k], s1.at[k], r1.at[k], "bus", peer)

    def start1(k, carry):
        send1(k).start()
        return carry

    lax.fori_loop(1, n_bus, start1, 0)
    held[here] = rows_ref[...]
    advance(big, 2, pieces)
    total = x_ref[pl.ds(me * chunk, chunk), :]

    def finish1(k, acc):
        send1(k).wait()
        return acc + recv[k]

    total = lax.fori_loop(1, n_bus, finish1, total)
    gathered[pl.ds(me * chunk, chunk), :] = total
    mine[...] = total

    def send2(k):
        peer = lax.rem(me + k, n_bus)
        return _remote(mine, gathered.at[pl.ds(me * chunk, chunk)], s2.at[k], r2.at[k], "bus", peer)

    def start2(k, carry):
        send2(k).start()
        return carry

    lax.fori_loop(1, n_bus, start2, 0)
    advance(big, 3, pieces)

    def finish2(k, carry):
        send2(k).wait()
        return carry

    lax.fori_loop(1, n_bus, finish2, 0)

    for i in range(picked.shape[0]):
        picked[pl.ds(i, 1), :] = gathered[pl.ds(pick_ref[i], 1), :]
    got[here] = picked[...]
    advance(small, 1, 1)
    next_small = 2
    for step in range(4, to_right + 1):
        advance(big, step, pieces)
        advance(small, next_small, 1)
        next_small += 1
    for step in range(next_small, to_right + 1):
        advance(small, step, 1)
    drain(big, pieces)
    drain(small, 1)
    o_ref[...] = gathered[...]
    o_rows[...] = held[...]
    o_small[...] = got[...]


def exchange(pick, factors, ends, rows, n_bus, n_line, pieces=2):
    x = jax.ShapeDtypeStruct((factors.shape[0], ends.shape[1]), factors.dtype)
    x_rows, x_cols = x.shape
    chunk = x_rows // n_bus
    vmem = pl.BlockSpec(memory_space=pltpu.VMEM)
    smem = pl.BlockSpec(memory_space=pltpu.SMEM)
    held_shape = (n_line,) + rows.shape
    got_shape = (n_line, pick.shape[0], x_cols)
    return pl.pallas_call(
        functools.partial(_exchange_kernel, n_bus, n_line, pieces),
        out_shape=(
            jax.ShapeDtypeStruct(x.shape, x.dtype),
            jax.ShapeDtypeStruct(held_shape, rows.dtype),
            jax.ShapeDtypeStruct(got_shape, x.dtype),
        ),
        in_specs=[smem, vmem, vmem, vmem],
        out_specs=(vmem, vmem, vmem),
        scratch_shapes=[
            pltpu.VMEM(x.shape, x.dtype),
            pltpu.VMEM((n_bus, chunk, x_cols), x.dtype),
            pltpu.VMEM(x.shape, x.dtype),
            pltpu.VMEM((chunk, x_cols), x.dtype),
            pltpu.VMEM(held_shape, rows.dtype),
            pltpu.VMEM((pick.shape[0], x_cols), x.dtype),
            pltpu.VMEM(got_shape, x.dtype),
        ]
        + [pltpu.SemaphoreType.DMA((n_bus,))] * 4
        + [pltpu.SemaphoreType.DMA((n_line * pieces,))] * 4
        + [pltpu.SemaphoreType.DMA((n_line,))] * 4,
        compiler_params=pltpu.CompilerParams(
            collective_id=0, has_side_effects=True, vmem_limit_bytes=48 * 1024 * 1024
        ),
    )(pick, factors, ends, rows)


def chol_solve(factor_lower, right):
    middle = lax.linalg.triangular_solve(factor_lower, right, left_side=True, lower=True)
    return lax.linalg.triangular_solve(
        factor_lower, middle, left_side=True, lower=True, transpose_a=True
    )


def solve_weights(capacitance, terminal_rows):
    factor_lower = jnp.linalg.cholesky(jnp.dot(capacitance, capacitance.T, precision=PRECISE))
    return chol_solve(factor_lower, jnp.dot(capacitance, terminal_rows.T, precision=PRECISE))


def slot_layout(tripped, local_rows, cap):
    steps, outages = tripped.shape
    block = tripped // local_rows
    earlier = jnp.arange(outages)[None, :] < jnp.arange(outages)[:, None]
    same = (block[:, :, None] == block[:, None, :]) & earlier[None]
    rank = jnp.sum(same, axis=2).astype(jnp.int32)
    seg = jnp.arange(steps, dtype=jnp.int32)[:, None]
    slot = block * (steps * cap) + seg * cap + rank
    return block, rank, slot


def per_device(transfer_factors, line_flows, from_bus, to_bus, tripped):
    local_rows, local_cols = transfer_factors.shape
    steps, outages = tripped.shape
    cap = 8
    line_index = lax.axis_index("line")
    bus_index = lax.axis_index("bus")
    ids = tripped.reshape(-1)

    def local_column(bus):
        offset = bus - bus_index * local_cols
        return jnp.where((offset >= 0) & (offset < local_cols), offset, -1)

    ends = jnp.stack([local_column(jnp.take(from_bus, ids)), local_column(jnp.take(to_bus, ids))])

    block, rank, slot = slot_layout(tripped, local_rows, cap)
    mine = (block == line_index)[:, None, :] & (
        rank[:, None, :] == jnp.arange(cap, dtype=jnp.int32)[None, :, None]
    )
    position = jnp.sum(jnp.where(mine, (tripped - line_index * local_rows)[:, None, :], 0), axis=2)
    valid = jnp.any(mine, axis=2).reshape(-1)
    position = position.reshape(-1)
    rows = jnp.take(transfer_factors, position, axis=0)
    flows = jnp.take(line_flows, position)
    extra = jnp.zeros((position.shape[0], 128), jnp.float32).at[:, 0].set(flows)
    rows = jnp.where(valid[:, None], jnp.concatenate([rows, extra], axis=1), 0.0)
    pick = jnp.where(valid, position, 0).astype(jnp.int32)
    terminal, gathered_rows, gathered_small = exchange(
        pick, transfer_factors, ends, rows, lax.axis_size("bus"), lax.axis_size("line")
    )
    gathered_rows = gathered_rows.reshape(-1, rows.shape[1])
    gathered_small = gathered_small.reshape(-1, terminal.shape[1])
    slot_flat = slot.reshape(-1)
    outage_all = jnp.take(gathered_rows, slot_flat, axis=0)
    outage_rows = outage_all[:, :local_cols]
    outage_flows = outage_all[:, local_cols]
    outage_terms = jnp.take(gathered_small, slot_flat, axis=0)

    identity = jnp.eye(outages, dtype=jnp.float32)
    row_global = line_index * local_rows + jnp.arange(local_rows, dtype=jnp.int32)
    hit = row_global[:, None] == tripped[0][None, :]
    keep1 = 1.0 - jnp.any(hit, axis=1).astype(jnp.float32)
    hit2 = row_global[:, None] == tripped[1][None, :]
    keep12 = keep1 * (1.0 - jnp.any(hit2, axis=1).astype(jnp.float32))

    s1 = slice(0, outages)
    s2 = slice(outages, 2 * outages)
    cap1 = identity - outage_terms[s1, s1]
    rhs1 = jnp.concatenate([terminal[:, s1], outage_terms[s2, s1]], axis=0)
    w1 = solve_weights(cap1, rhs1)
    w1t_local = w1[:, :local_rows].T
    w1t_out2 = w1[:, local_rows:].T
    terminal2 = keep1[:, None] * (
        terminal[:, s2] + jnp.dot(w1t_local, outage_terms[s1, s2], precision=PRECISE)
    )
    out2 = outage_terms[s2, s2] + jnp.dot(w1t_out2, outage_terms[s1, s2], precision=PRECISE)
    cap2 = identity - out2
    w2t = solve_weights(cap2, terminal2).T
    combined = jnp.concatenate(
        [w1t_local + jnp.dot(w2t, w1t_out2, precision=PRECISE), w2t], axis=1
    )

    factors = keep12[:, None] * (
        transfer_factors + jnp.dot(combined, outage_rows, precision=PRECISE)
    )
    flows = keep12 * (line_flows + jnp.dot(combined, outage_flows, precision=PRECISE))
    return (factors, flows)


def solution(mesh):
    placed = (P("line", "bus"), P("line"), P(), P(), P())
    return jax.shard_map(
        per_device,
        mesh=mesh,
        in_specs=placed,
        out_specs=(P("line", "bus"), P("line")),
        check_vma=False,
    )
```

```python
import functools

import jax
import jax.numpy as jnp
from jax import lax
from jax.experimental import pallas as pl
from jax.experimental.pallas import tpu as pltpu
from jax.sharding import PartitionSpec as P

PRECISE = lax.Precision.HIGHEST


def _mesh_id(axis, peer):
    coords = {"line": lax.axis_index("line"), "bus": lax.axis_index("bus")}
    coords[axis] = peer
    return (coords["line"], coords["bus"])


def _greet(axis, n):
    barrier = pltpu.get_barrier_semaphore()
    me = lax.axis_index(axis)

    def body(k, carry):
        peer = lax.rem(me + k, n)
        pl.semaphore_signal(
            barrier, 1, device_id=_mesh_id(axis, peer), device_id_type=pl.DeviceIdType.MESH
        )
        return carry

    lax.fori_loop(1, n, body, 0)
    pl.semaphore_wait(barrier, n - 1)


def _remote(src, dst, send_sem, recv_sem, axis, peer):
    return pltpu.make_async_remote_copy(
        src_ref=src,
        dst_ref=dst,
        send_sem=send_sem,
        recv_sem=recv_sem,
        device_id=_mesh_id(axis, peer),
        device_id_type=pl.DeviceIdType.MESH,
    )


def _exchange_kernel(
    n_bus, n_line, pieces, pick_ref, p_ref, ends_ref, rows_ref, extra_ref, o_ref, o_rows, o_small,
    x_ref, recv, gathered, mine, held, picked, got, s1, r1, s2, r2, sr, rr, sl, rl,
    tsr, trr, tsl, trl,
):
    me = lax.axis_index("bus")
    here = lax.axis_index("line")
    right = lax.rem(here + 1, n_line)
    left = lax.rem(here + n_line - 1, n_line)
    chunk = x_ref.shape[0] // n_bus
    piece = rows_ref.shape[0] // pieces
    to_right = n_line // 2
    to_left = n_line - 1 - to_right
    mesh_type = pl.DeviceIdType.MESH

    barrier = pltpu.get_barrier_semaphore()

    def greet_bus(k, carry):
        pl.semaphore_signal(
            barrier, 1, device_id=_mesh_id("bus", lax.rem(me + k, n_bus)), device_id_type=mesh_type
        )
        return carry

    lax.fori_loop(1, n_bus, greet_bus, 0)
    for neighbour in (left, right):
        pl.semaphore_signal(
            barrier, 1, device_id=_mesh_id("line", neighbour), device_id_type=mesh_type
        )
    pl.semaphore_wait(barrier, n_bus - 1 + 2)

    def ring_steps(toward):
        return to_right if toward == "right" else to_left

    def ring_copy(step, part, toward, first, buf, parts, sems):
        send_right, recv_right, send_left, recv_left = sems
        if toward == "right":
            origin = lax.rem(here - (step - 1) + n_line, n_line)
            peer, send_sem, recv_sem = right, send_right, recv_right
        else:
            origin = lax.rem(here + (step - 1), n_line)
            peer, send_sem, recv_sem = left, send_left, recv_left
        size = first.shape[0] // parts
        rows = pl.ds(part * size, size)
        src = first.at[rows] if step == 1 else buf.at[origin, rows]
        slot = (step - 1) * parts + part
        return _remote(src, buf.at[origin, rows], send_sem.at[slot], recv_sem.at[slot], "line", peer)

    def big(step):
        return lambda part, toward: ring_copy(step, part, toward, rows_ref, held, pieces, (sr, rr, sl, rl))

    def small(step):
        return lambda part, toward: ring_copy(step, part, toward, picked, got, 1, (tsr, trr, tsl, trl))

    def advance(copies, step, parts):
        for part in range(parts):
            for toward in ("right", "left"):
                if step <= ring_steps(toward):
                    if step > 1:
                        copies(step - 1)(part, toward).wait_recv()
                    copies(step)(part, toward).start()

    def drain(copies, parts):
        for toward in ("right", "left"):
            last = ring_steps(toward)
            for part in range(parts):
                if last >= 1:
                    copies(last)(part, toward).wait_recv()
            for step in range(1, last + 1):
                for part in range(parts):
                    copies(step)(part, toward).wait_send()

    advance(big, 1, pieces)

    local_cols = p_ref.shape[1]
    column = lax.broadcasted_iota(jnp.int32, (local_cols, ends_ref.shape[1]), 0)
    select = (column == ends_ref[0:1, :]).astype(jnp.float32) - (
        column == ends_ref[1:2, :]
    ).astype(jnp.float32)
    x_ref[...] = jnp.dot(
        p_ref[...], select, precision=PRECISE, preferred_element_type=jnp.float32
    )

    def send1(k):
        peer = lax.rem(me + k, n_bus)
        return _remote(x_ref.at[pl.ds(peer * chunk, chunk)], recv.at[k], s1.at[k], r1.at[k], "bus", peer)

    def start1(k, carry):
        send1(k).start()
        return carry

    lax.fori_loop(1, n_bus, start1, 0)
    held[here] = rows_ref[...]
    advance(big, 2, pieces)
    total = x_ref[pl.ds(me * chunk, chunk), :]

    def finish1(k, acc):
        send1(k).wait()
        return acc + recv[k]

    total = lax.fori_loop(1, n_bus, finish1, total)
    gathered[pl.ds(me * chunk, chunk), :] = total
    mine[...] = total

    def send2(k):
        peer = lax.rem(me + k, n_bus)
        return _remote(mine, gathered.at[pl.ds(me * chunk, chunk)], s2.at[k], r2.at[k], "bus", peer)

    def start2(k, carry):
        send2(k).start()
        return carry

    lax.fori_loop(1, n_bus, start2, 0)
    advance(big, 3, pieces)

    def finish2(k, carry):
        send2(k).wait()
        return carry

    lax.fori_loop(1, n_bus, finish2, 0)

    width = gathered.shape[1]
    for i in range(picked.shape[0]):
        picked[pl.ds(i, 1), :width] = gathered[pl.ds(pick_ref[i], 1), :]
    picked[:, width:] = extra_ref[...]
    got[here] = picked[...]
    advance(small, 1, 1)
    next_small = 2
    for step in range(4, to_right + 1):
        advance(big, step, pieces)
        advance(small, next_small, 1)
        next_small += 1
    for step in range(next_small, to_right + 1):
        advance(small, step, 1)
    drain(big, pieces)
    drain(small, 1)
    o_ref[...] = gathered[...]
    o_rows[...] = held[...]
    o_small[...] = got[...]


def exchange(pick, factors, ends, rows, extra, n_bus, n_line, pieces=4):
    x = jax.ShapeDtypeStruct((factors.shape[0], ends.shape[1]), factors.dtype)
    x_rows, x_cols = x.shape
    chunk = x_rows // n_bus
    vmem = pl.BlockSpec(memory_space=pltpu.VMEM)
    smem = pl.BlockSpec(memory_space=pltpu.SMEM)
    held_shape = (n_line,) + rows.shape
    got_shape = (n_line, pick.shape[0], x_cols + extra.shape[1])
    return pl.pallas_call(
        functools.partial(_exchange_kernel, n_bus, n_line, pieces),
        out_shape=(
            jax.ShapeDtypeStruct(x.shape, x.dtype),
            jax.ShapeDtypeStruct(held_shape, rows.dtype),
            jax.ShapeDtypeStruct(got_shape, x.dtype),
        ),
        in_specs=[smem, vmem, vmem, vmem, vmem],
        out_specs=(vmem, vmem, vmem),
        scratch_shapes=[
            pltpu.VMEM(x.shape, x.dtype),
            pltpu.VMEM((n_bus, chunk, x_cols), x.dtype),
            pltpu.VMEM(x.shape, x.dtype),
            pltpu.VMEM((chunk, x_cols), x.dtype),
            pltpu.VMEM(held_shape, rows.dtype),
            pltpu.VMEM((pick.shape[0], x_cols + extra.shape[1]), x.dtype),
            pltpu.VMEM(got_shape, x.dtype),
        ]
        + [pltpu.SemaphoreType.DMA((n_bus,))] * 4
        + [pltpu.SemaphoreType.DMA((n_line * pieces,))] * 4
        + [pltpu.SemaphoreType.DMA((n_line,))] * 4,
        compiler_params=pltpu.CompilerParams(
            collective_id=0, has_side_effects=True, vmem_limit_bytes=48 * 1024 * 1024
        ),
    )(pick, factors, ends, rows, extra)


def chol_solve(factor_lower, right):
    middle = lax.linalg.triangular_solve(factor_lower, right, left_side=True, lower=True)
    return lax.linalg.triangular_solve(
        factor_lower, middle, left_side=True, lower=True, transpose_a=True
    )


def solve_weights(capacitance, terminal_rows):
    factor_lower = jnp.linalg.cholesky(jnp.dot(capacitance, capacitance.T, precision=PRECISE))
    return chol_solve(factor_lower, jnp.dot(capacitance, terminal_rows.T, precision=PRECISE))


def slot_layout(tripped, local_rows, cap):
    steps, outages = tripped.shape
    block = tripped // local_rows
    earlier = jnp.arange(outages)[None, :] < jnp.arange(outages)[:, None]
    same = (block[:, :, None] == block[:, None, :]) & earlier[None]
    rank = jnp.sum(same, axis=2).astype(jnp.int32)
    seg = jnp.arange(steps, dtype=jnp.int32)[:, None]
    slot = block * (steps * cap) + seg * cap + rank
    return block, rank, slot


def per_device(transfer_factors, line_flows, from_bus, to_bus, tripped):
    local_rows, local_cols = transfer_factors.shape
    steps, outages = tripped.shape
    cap = 8
    line_index = lax.axis_index("line")
    bus_index = lax.axis_index("bus")
    ids = tripped.reshape(-1)

    def local_column(bus):
        offset = bus - bus_index * local_cols
        return jnp.where((offset >= 0) & (offset < local_cols), offset, -1)

    ends = jnp.stack([local_column(jnp.take(from_bus, ids)), local_column(jnp.take(to_bus, ids))])

    block, rank, slot = slot_layout(tripped, local_rows, cap)
    mine = (block == line_index)[:, None, :] & (
        rank[:, None, :] == jnp.arange(cap, dtype=jnp.int32)[None, :, None]
    )
    position = jnp.sum(jnp.where(mine, (tripped - line_index * local_rows)[:, None, :], 0), axis=2)
    valid = jnp.any(mine, axis=2).reshape(-1)
    position = position.reshape(-1)
    rows = jnp.take(transfer_factors, position, axis=0)
    flows = jnp.take(line_flows, position)
    extra = jnp.zeros((position.shape[0], 128), jnp.float32).at[:, 0].set(flows)
    rows = jnp.where(valid[:, None], rows, 0.0)
    pick = jnp.where(valid, position, 0).astype(jnp.int32)
    terminal, gathered_rows, gathered_small = exchange(
        pick, transfer_factors, ends, rows, extra, lax.axis_size("bus"), lax.axis_size("line")
    )
    gathered_rows = gathered_rows.reshape(-1, rows.shape[1])
    gathered_small = gathered_small.reshape(-1, gathered_small.shape[-1])
    slot_flat = slot.reshape(-1)
    outage_rows = jnp.take(gathered_rows, slot_flat, axis=0)
    outage_small = jnp.take(gathered_small, slot_flat, axis=0)
    outage_terms = outage_small[:, : terminal.shape[1]]
    outage_flows = outage_small[:, terminal.shape[1]]

    identity = jnp.eye(outages, dtype=jnp.float32)
    row_global = line_index * local_rows + jnp.arange(local_rows, dtype=jnp.int32)
    hit = row_global[:, None] == tripped[0][None, :]
    keep1 = 1.0 - jnp.any(hit, axis=1).astype(jnp.float32)
    hit2 = row_global[:, None] == tripped[1][None, :]
    keep12 = keep1 * (1.0 - jnp.any(hit2, axis=1).astype(jnp.float32))

    s1 = slice(0, outages)
    s2 = slice(outages, 2 * outages)
    cap1 = identity - outage_terms[s1, s1]
    rhs1 = jnp.concatenate([terminal[:, s1], outage_terms[s2, s1]], axis=0)
    w1 = solve_weights(cap1, rhs1)
    w1t_local = w1[:, :local_rows].T
    w1t_out2 = w1[:, local_rows:].T
    terminal2 = keep1[:, None] * (
        terminal[:, s2] + jnp.dot(w1t_local, outage_terms[s1, s2], precision=PRECISE)
    )
    out2 = outage_terms[s2, s2] + jnp.dot(w1t_out2, outage_terms[s1, s2], precision=PRECISE)
    cap2 = identity - out2
    w2t = solve_weights(cap2, terminal2).T
    combined = jnp.concatenate(
        [w1t_local + jnp.dot(w2t, w1t_out2, precision=PRECISE), w2t], axis=1
    )

    factors = keep12[:, None] * (
        transfer_factors + jnp.dot(combined, outage_rows, precision=PRECISE)
    )
    flows = keep12 * (line_flows + jnp.dot(combined, outage_flows, precision=PRECISE))
    return (factors, flows)


def solution(mesh):
    placed = (P("line", "bus"), P("line"), P(), P(), P())
    return jax.shard_map(
        per_device,
        mesh=mesh,
        in_specs=placed,
        out_specs=(P("line", "bus"), P("line")),
        check_vma=False,
    )
```

```python
import functools

import jax
import jax.numpy as jnp
from jax import lax
from jax.experimental import pallas as pl
from jax.experimental.pallas import tpu as pltpu
from jax.sharding import PartitionSpec as P

PRECISE = lax.Precision.HIGHEST


def _mesh_id(axis, peer):
    coords = {"line": lax.axis_index("line"), "bus": lax.axis_index("bus")}
    coords[axis] = peer
    return (coords["line"], coords["bus"])


def _greet(axis, n):
    barrier = pltpu.get_barrier_semaphore()
    me = lax.axis_index(axis)

    def body(k, carry):
        peer = lax.rem(me + k, n)
        pl.semaphore_signal(
            barrier, 1, device_id=_mesh_id(axis, peer), device_id_type=pl.DeviceIdType.MESH
        )
        return carry

    lax.fori_loop(1, n, body, 0)
    pl.semaphore_wait(barrier, n - 1)


def _remote(src, dst, send_sem, recv_sem, axis, peer):
    return pltpu.make_async_remote_copy(
        src_ref=src,
        dst_ref=dst,
        send_sem=send_sem,
        recv_sem=recv_sem,
        device_id=_mesh_id(axis, peer),
        device_id_type=pl.DeviceIdType.MESH,
    )


def _exchange_kernel(
    n_bus, n_line, pieces, pick_ref, p_ref, ends_ref, extra_ref, o_ref, o_rows, o_small,
    rows_ref, x_ref, recv, gathered, mine, held, picked, got, s1, r1, s2, r2, sr, rr, sl, rl,
    tsr, trr, tsl, trl,
):
    me = lax.axis_index("bus")
    here = lax.axis_index("line")
    right = lax.rem(here + 1, n_line)
    left = lax.rem(here + n_line - 1, n_line)
    chunk = x_ref.shape[0] // n_bus
    piece = rows_ref.shape[0] // pieces
    to_right = n_line // 2
    to_left = n_line - 1 - to_right
    mesh_type = pl.DeviceIdType.MESH

    barrier = pltpu.get_barrier_semaphore()

    def greet_bus(k, carry):
        pl.semaphore_signal(
            barrier, 1, device_id=_mesh_id("bus", lax.rem(me + k, n_bus)), device_id_type=mesh_type
        )
        return carry

    lax.fori_loop(1, n_bus, greet_bus, 0)
    for neighbour in (left, right):
        pl.semaphore_signal(
            barrier, 1, device_id=_mesh_id("line", neighbour), device_id_type=mesh_type
        )
    pl.semaphore_wait(barrier, n_bus - 1 + 2)

    def ring_steps(toward):
        return to_right if toward == "right" else to_left

    def ring_copy(step, part, toward, first, buf, parts, sems):
        send_right, recv_right, send_left, recv_left = sems
        if toward == "right":
            origin = lax.rem(here - (step - 1) + n_line, n_line)
            peer, send_sem, recv_sem = right, send_right, recv_right
        else:
            origin = lax.rem(here + (step - 1), n_line)
            peer, send_sem, recv_sem = left, send_left, recv_left
        size = first.shape[0] // parts
        rows = pl.ds(part * size, size)
        src = first.at[rows] if step == 1 else buf.at[origin, rows]
        slot = (step - 1) * parts + part
        return _remote(src, buf.at[origin, rows], send_sem.at[slot], recv_sem.at[slot], "line", peer)

    def big(step):
        return lambda part, toward: ring_copy(step, part, toward, rows_ref, held, pieces, (sr, rr, sl, rl))

    def small(step):
        return lambda part, toward: ring_copy(step, part, toward, picked, got, 1, (tsr, trr, tsl, trl))

    def advance(copies, step, parts):
        for part in range(parts):
            for toward in ("right", "left"):
                if step <= ring_steps(toward):
                    if step > 1:
                        copies(step - 1)(part, toward).wait_recv()
                    copies(step)(part, toward).start()

    def drain(copies, parts):
        for toward in ("right", "left"):
            last = ring_steps(toward)
            for part in range(parts):
                if last >= 1:
                    copies(last)(part, toward).wait_recv()
            for step in range(1, last + 1):
                for part in range(parts):
                    copies(step)(part, toward).wait_send()

    for i in range(rows_ref.shape[0]):
        rows_ref[pl.ds(i, 1), :] = p_ref[pl.ds(pick_ref[i], 1), :]
    advance(big, 1, pieces)

    local_cols = p_ref.shape[1]
    column = lax.broadcasted_iota(jnp.int32, (local_cols, ends_ref.shape[1]), 0)
    select = (column == ends_ref[0:1, :]).astype(jnp.float32) - (
        column == ends_ref[1:2, :]
    ).astype(jnp.float32)
    x_ref[...] = jnp.dot(
        p_ref[...], select, precision=PRECISE, preferred_element_type=jnp.float32
    )

    def send1(k):
        peer = lax.rem(me + k, n_bus)
        return _remote(x_ref.at[pl.ds(peer * chunk, chunk)], recv.at[k], s1.at[k], r1.at[k], "bus", peer)

    def start1(k, carry):
        send1(k).start()
        return carry

    lax.fori_loop(1, n_bus, start1, 0)
    held[here] = rows_ref[...]
    advance(big, 2, pieces)
    total = x_ref[pl.ds(me * chunk, chunk), :]

    def finish1(k, acc):
        send1(k).wait()
        return acc + recv[k]

    total = lax.fori_loop(1, n_bus, finish1, total)
    gathered[pl.ds(me * chunk, chunk), :] = total
    mine[...] = total

    def send2(k):
        peer = lax.rem(me + k, n_bus)
        return _remote(mine, gathered.at[pl.ds(me * chunk, chunk)], s2.at[k], r2.at[k], "bus", peer)

    def start2(k, carry):
        send2(k).start()
        return carry

    lax.fori_loop(1, n_bus, start2, 0)
    advance(big, 3, pieces)

    def finish2(k, carry):
        send2(k).wait()
        return carry

    lax.fori_loop(1, n_bus, finish2, 0)

    width = gathered.shape[1]
    for i in range(picked.shape[0]):
        picked[pl.ds(i, 1), :width] = gathered[pl.ds(pick_ref[i], 1), :]
    picked[:, width:] = extra_ref[...]
    got[here] = picked[...]
    advance(small, 1, 1)
    next_small = 2
    for step in range(4, to_right + 1):
        advance(big, step, pieces)
        advance(small, next_small, 1)
        next_small += 1
    for step in range(next_small, to_right + 1):
        advance(small, step, 1)
    drain(big, pieces)
    drain(small, 1)
    o_ref[...] = gathered[...]
    o_rows[...] = held[...]
    o_small[...] = got[...]


def exchange(pick, factors, ends, extra, n_bus, n_line, pieces=4):
    rows = jax.ShapeDtypeStruct((pick.shape[0], factors.shape[1]), factors.dtype)
    x = jax.ShapeDtypeStruct((factors.shape[0], ends.shape[1]), factors.dtype)
    x_rows, x_cols = x.shape
    chunk = x_rows // n_bus
    vmem = pl.BlockSpec(memory_space=pltpu.VMEM)
    smem = pl.BlockSpec(memory_space=pltpu.SMEM)
    held_shape = (n_line,) + rows.shape
    got_shape = (n_line, pick.shape[0], x_cols + extra.shape[1])
    return pl.pallas_call(
        functools.partial(_exchange_kernel, n_bus, n_line, pieces),
        out_shape=(
            jax.ShapeDtypeStruct(x.shape, x.dtype),
            jax.ShapeDtypeStruct(held_shape, rows.dtype),
            jax.ShapeDtypeStruct(got_shape, x.dtype),
        ),
        in_specs=[smem, vmem, vmem, vmem],
        out_specs=(vmem, vmem, vmem),
        scratch_shapes=[
            pltpu.VMEM(rows.shape, rows.dtype),
            pltpu.VMEM(x.shape, x.dtype),
            pltpu.VMEM((n_bus, chunk, x_cols), x.dtype),
            pltpu.VMEM(x.shape, x.dtype),
            pltpu.VMEM((chunk, x_cols), x.dtype),
            pltpu.VMEM(held_shape, rows.dtype),
            pltpu.VMEM((pick.shape[0], x_cols + extra.shape[1]), x.dtype),
            pltpu.VMEM(got_shape, x.dtype),
        ]
        + [pltpu.SemaphoreType.DMA((n_bus,))] * 4
        + [pltpu.SemaphoreType.DMA((n_line * pieces,))] * 4
        + [pltpu.SemaphoreType.DMA((n_line,))] * 4,
        compiler_params=pltpu.CompilerParams(
            collective_id=0, has_side_effects=True, vmem_limit_bytes=48 * 1024 * 1024
        ),
    )(pick, factors, ends, extra)


def chol_solve(factor_lower, right):
    middle = lax.linalg.triangular_solve(factor_lower, right, left_side=True, lower=True)
    return lax.linalg.triangular_solve(
        factor_lower, middle, left_side=True, lower=True, transpose_a=True
    )


def solve_weights(capacitance, terminal_rows):
    factor_lower = jnp.linalg.cholesky(jnp.dot(capacitance, capacitance.T, precision=PRECISE))
    return chol_solve(factor_lower, jnp.dot(capacitance, terminal_rows.T, precision=PRECISE))


def slot_layout(tripped, local_rows, cap):
    steps, outages = tripped.shape
    block = tripped // local_rows
    earlier = jnp.arange(outages)[None, :] < jnp.arange(outages)[:, None]
    same = (block[:, :, None] == block[:, None, :]) & earlier[None]
    rank = jnp.sum(same, axis=2).astype(jnp.int32)
    seg = jnp.arange(steps, dtype=jnp.int32)[:, None]
    slot = block * (steps * cap) + seg * cap + rank
    return block, rank, slot


def per_device(transfer_factors, line_flows, from_bus, to_bus, tripped):
    local_rows, local_cols = transfer_factors.shape
    steps, outages = tripped.shape
    cap = 8
    line_index = lax.axis_index("line")
    bus_index = lax.axis_index("bus")
    ids = tripped.reshape(-1)

    def local_column(bus):
        offset = bus - bus_index * local_cols
        return jnp.where((offset >= 0) & (offset < local_cols), offset, -1)

    ends = jnp.stack([local_column(jnp.take(from_bus, ids)), local_column(jnp.take(to_bus, ids))])

    block, rank, slot = slot_layout(tripped, local_rows, cap)
    mine = (block == line_index)[:, None, :] & (
        rank[:, None, :] == jnp.arange(cap, dtype=jnp.int32)[None, :, None]
    )
    position = jnp.sum(jnp.where(mine, (tripped - line_index * local_rows)[:, None, :], 0), axis=2)
    valid = jnp.any(mine, axis=2).reshape(-1)
    position = position.reshape(-1)
    flows = jnp.take(line_flows, position)
    extra = jnp.zeros((position.shape[0], 128), jnp.float32).at[:, 0].set(flows)
    pick = jnp.where(valid, position, 0).astype(jnp.int32)
    terminal, gathered_rows, gathered_small = exchange(
        pick, transfer_factors, ends, extra, lax.axis_size("bus"), lax.axis_size("line")
    )
    gathered_rows = gathered_rows.reshape(-1, local_cols)
    gathered_small = gathered_small.reshape(-1, gathered_small.shape[-1])
    slot_flat = slot.reshape(-1)
    outage_rows = jnp.take(gathered_rows, slot_flat, axis=0)
    outage_small = jnp.take(gathered_small, slot_flat, axis=0)
    outage_terms = outage_small[:, : terminal.shape[1]]
    outage_flows = outage_small[:, terminal.shape[1]]

    identity = jnp.eye(outages, dtype=jnp.float32)
    row_global = line_index * local_rows + jnp.arange(local_rows, dtype=jnp.int32)
    hit = row_global[:, None] == tripped[0][None, :]
    keep1 = 1.0 - jnp.any(hit, axis=1).astype(jnp.float32)
    hit2 = row_global[:, None] == tripped[1][None, :]
    keep12 = keep1 * (1.0 - jnp.any(hit2, axis=1).astype(jnp.float32))

    s1 = slice(0, outages)
    s2 = slice(outages, 2 * outages)
    cap1 = identity - outage_terms[s1, s1]
    rhs1 = jnp.concatenate([terminal[:, s1], outage_terms[s2, s1]], axis=0)
    w1 = solve_weights(cap1, rhs1)
    w1t_local = w1[:, :local_rows].T
    w1t_out2 = w1[:, local_rows:].T
    terminal2 = keep1[:, None] * (
        terminal[:, s2] + jnp.dot(w1t_local, outage_terms[s1, s2], precision=PRECISE)
    )
    out2 = outage_terms[s2, s2] + jnp.dot(w1t_out2, outage_terms[s1, s2], precision=PRECISE)
    cap2 = identity - out2
    w2t = solve_weights(cap2, terminal2).T
    combined = jnp.concatenate(
        [w1t_local + jnp.dot(w2t, w1t_out2, precision=PRECISE), w2t], axis=1
    )

    factors = keep12[:, None] * (
        transfer_factors + jnp.dot(combined, outage_rows, precision=PRECISE)
    )
    flows = keep12 * (line_flows + jnp.dot(combined, outage_flows, precision=PRECISE))
    return (factors, flows)


def solution(mesh):
    placed = (P("line", "bus"), P("line"), P(), P(), P())
    return jax.shard_map(
        per_device,
        mesh=mesh,
        in_specs=placed,
        out_specs=(P("line", "bus"), P("line")),
        check_vma=False,
    )
```

```python
import functools

import jax
import jax.numpy as jnp
from jax import lax
from jax.experimental import pallas as pl
from jax.experimental.pallas import tpu as pltpu
from jax.sharding import PartitionSpec as P

PRECISE = lax.Precision.HIGHEST


def _mesh_id(axis, peer):
    coords = {"line": lax.axis_index("line"), "bus": lax.axis_index("bus")}
    coords[axis] = peer
    return (coords["line"], coords["bus"])


def _greet(axis, n):
    barrier = pltpu.get_barrier_semaphore()
    me = lax.axis_index(axis)

    def body(k, carry):
        peer = lax.rem(me + k, n)
        pl.semaphore_signal(
            barrier, 1, device_id=_mesh_id(axis, peer), device_id_type=pl.DeviceIdType.MESH
        )
        return carry

    lax.fori_loop(1, n, body, 0)
    pl.semaphore_wait(barrier, n - 1)


def _remote(src, dst, send_sem, recv_sem, axis, peer):
    return pltpu.make_async_remote_copy(
        src_ref=src,
        dst_ref=dst,
        send_sem=send_sem,
        recv_sem=recv_sem,
        device_id=_mesh_id(axis, peer),
        device_id_type=pl.DeviceIdType.MESH,
    )


def _exchange_kernel(
    n_bus, n_line, pieces, pick_ref, p_ref, ends_ref, rows_ref, o_ref, o_rows, o_small,
    x_ref, recv, gathered, mine, held, picked, got, s1, r1, s2, r2, sr, rr, sl, rl,
    tsr, trr, tsl, trl,
):
    me = lax.axis_index("bus")
    here = lax.axis_index("line")
    right = lax.rem(here + 1, n_line)
    left = lax.rem(here + n_line - 1, n_line)
    chunk = x_ref.shape[0] // n_bus
    piece = rows_ref.shape[0] // pieces
    to_right = n_line // 2
    to_left = n_line - 1 - to_right
    mesh_type = pl.DeviceIdType.MESH

    barrier = pltpu.get_barrier_semaphore()

    def greet_bus(k, carry):
        pl.semaphore_signal(
            barrier, 1, device_id=_mesh_id("bus", lax.rem(me + k, n_bus)), device_id_type=mesh_type
        )
        return carry

    lax.fori_loop(1, n_bus, greet_bus, 0)
    for neighbour in (left, right):
        pl.semaphore_signal(
            barrier, 1, device_id=_mesh_id("line", neighbour), device_id_type=mesh_type
        )
    pl.semaphore_wait(barrier, n_bus - 1 + 2)

    def ring_steps(toward):
        return to_right if toward == "right" else to_left

    def ring_copy(step, part, toward, first, buf, parts, sems):
        send_right, recv_right, send_left, recv_left = sems
        if toward == "right":
            origin = lax.rem(here - (step - 1) + n_line, n_line)
            peer, send_sem, recv_sem = right, send_right, recv_right
        else:
            origin = lax.rem(here + (step - 1), n_line)
            peer, send_sem, recv_sem = left, send_left, recv_left
        size = first.shape[0] // parts
        rows = pl.ds(part * size, size)
        src = first.at[rows] if step == 1 else buf.at[origin, rows]
        slot = (step - 1) * parts + part
        return _remote(src, buf.at[origin, rows], send_sem.at[slot], recv_sem.at[slot], "line", peer)

    def big(step):
        return lambda part, toward: ring_copy(step, part, toward, rows_ref, held, pieces, (sr, rr, sl, rl))

    def small(step):
        return lambda part, toward: ring_copy(step, part, toward, picked, got, 1, (tsr, trr, tsl, trl))

    def advance(copies, step, parts):
        for part in range(parts):
            for toward in ("right", "left"):
                if step <= ring_steps(toward):
                    if step > 1:
                        copies(step - 1)(part, toward).wait_recv()
                    copies(step)(part, toward).start()

    def drain(copies, parts):
        for toward in ("right", "left"):
            last = ring_steps(toward)
            for part in range(parts):
                if last >= 1:
                    copies(last)(part, toward).wait_recv()
            for step in range(1, last + 1):
                for part in range(parts):
                    copies(step)(part, toward).wait_send()

    advance(big, 1, pieces)

    local_cols = p_ref.shape[1]
    column = lax.broadcasted_iota(jnp.int32, (local_cols, ends_ref.shape[1]), 0)
    select = (column == ends_ref[0:1, :]).astype(jnp.float32) - (
        column == ends_ref[1:2, :]
    ).astype(jnp.float32)
    x_ref[...] = jnp.dot(
        p_ref[...], select, precision=PRECISE, preferred_element_type=jnp.float32
    )

    def send1(k):
        peer = lax.rem(me + k, n_bus)
        return _remote(x_ref.at[pl.ds(peer * chunk, chunk)], recv.at[k], s1.at[k], r1.at[k], "bus", peer)

    def start1(k, carry):
        send1(k).start()
        return carry

    lax.fori_loop(1, n_bus, start1, 0)
    held[here] = rows_ref[...]
    advance(big, 2, pieces)
    total = x_ref[pl.ds(me * chunk, chunk), :]

    def finish1(k, acc):
        send1(k).wait()
        return acc + recv[k]

    total = lax.fori_loop(1, n_bus, finish1, total)
    gathered[pl.ds(me * chunk, chunk), :] = total
    mine[...] = total

    def send2(k):
        peer = lax.rem(me + k, n_bus)
        return _remote(mine, gathered.at[pl.ds(me * chunk, chunk)], s2.at[k], r2.at[k], "bus", peer)

    def start2(k, carry):
        send2(k).start()
        return carry

    lax.fori_loop(1, n_bus, start2, 0)
    advance(big, 3, pieces)

    def finish2(k, carry):
        send2(k).wait()
        return carry

    lax.fori_loop(1, n_bus, finish2, 0)

    for i in range(picked.shape[0]):
        picked[pl.ds(i, 1), :] = gathered[pl.ds(pick_ref[i], 1), :]
    got[here] = picked[...]
    advance(small, 1, 1)
    next_small = 2
    for step in range(4, to_right + 1):
        advance(big, step, pieces)
        for _ in range(2):
            if next_small <= to_right:
                advance(small, next_small, 1)
                next_small += 1
    for step in range(next_small, to_right + 1):
        advance(small, step, 1)
    drain(big, pieces)
    drain(small, 1)
    o_ref[...] = gathered[...]
    o_rows[...] = held[...]
    o_small[...] = got[...]


def exchange(pick, factors, ends, rows, n_bus, n_line, pieces=2):
    x = jax.ShapeDtypeStruct((factors.shape[0], ends.shape[1]), factors.dtype)
    x_rows, x_cols = x.shape
    chunk = x_rows // n_bus
    vmem = pl.BlockSpec(memory_space=pltpu.VMEM)
    smem = pl.BlockSpec(memory_space=pltpu.SMEM)
    held_shape = (n_line,) + rows.shape
    got_shape = (n_line, pick.shape[0], x_cols)
    return pl.pallas_call(
        functools.partial(_exchange_kernel, n_bus, n_line, pieces),
        out_shape=(
            jax.ShapeDtypeStruct(x.shape, x.dtype),
            jax.ShapeDtypeStruct(held_shape, rows.dtype),
            jax.ShapeDtypeStruct(got_shape, x.dtype),
        ),
        in_specs=[smem, vmem, vmem, vmem],
        out_specs=(vmem, vmem, vmem),
        scratch_shapes=[
            pltpu.VMEM(x.shape, x.dtype),
            pltpu.VMEM((n_bus, chunk, x_cols), x.dtype),
            pltpu.VMEM(x.shape, x.dtype),
            pltpu.VMEM((chunk, x_cols), x.dtype),
            pltpu.VMEM(held_shape, rows.dtype),
            pltpu.VMEM((pick.shape[0], x_cols), x.dtype),
            pltpu.VMEM(got_shape, x.dtype),
        ]
        + [pltpu.SemaphoreType.DMA((n_bus,))] * 4
        + [pltpu.SemaphoreType.DMA((n_line * pieces,))] * 4
        + [pltpu.SemaphoreType.DMA((n_line,))] * 4,
        compiler_params=pltpu.CompilerParams(
            collective_id=0, has_side_effects=True, vmem_limit_bytes=48 * 1024 * 1024
        ),
    )(pick, factors, ends, rows)


def chol_solve(factor_lower, right):
    middle = lax.linalg.triangular_solve(factor_lower, right, left_side=True, lower=True)
    return lax.linalg.triangular_solve(
        factor_lower, middle, left_side=True, lower=True, transpose_a=True
    )


def solve_weights(capacitance, terminal_rows):
    factor_lower = jnp.linalg.cholesky(jnp.dot(capacitance, capacitance.T, precision=PRECISE))
    return chol_solve(factor_lower, jnp.dot(capacitance, terminal_rows.T, precision=PRECISE))


def slot_layout(tripped, local_rows, cap):
    steps, outages = tripped.shape
    block = tripped // local_rows
    earlier = jnp.arange(outages)[None, :] < jnp.arange(outages)[:, None]
    same = (block[:, :, None] == block[:, None, :]) & earlier[None]
    rank = jnp.sum(same, axis=2).astype(jnp.int32)
    seg = jnp.arange(steps, dtype=jnp.int32)[:, None]
    slot = block * (steps * cap) + seg * cap + rank
    return block, rank, slot


def per_device(transfer_factors, line_flows, from_bus, to_bus, tripped):
    local_rows, local_cols = transfer_factors.shape
    steps, outages = tripped.shape
    cap = 8
    line_index = lax.axis_index("line")
    bus_index = lax.axis_index("bus")
    ids = tripped.reshape(-1)

    def local_column(bus):
        offset = bus - bus_index * local_cols
        return jnp.where((offset >= 0) & (offset < local_cols), offset, -1)

    ends = jnp.stack([local_column(jnp.take(from_bus, ids)), local_column(jnp.take(to_bus, ids))])

    block, rank, slot = slot_layout(tripped, local_rows, cap)
    mine = (block == line_index)[:, None, :] & (
        rank[:, None, :] == jnp.arange(cap, dtype=jnp.int32)[None, :, None]
    )
    position = jnp.sum(jnp.where(mine, (tripped - line_index * local_rows)[:, None, :], 0), axis=2)
    valid = jnp.any(mine, axis=2).reshape(-1)
    position = position.reshape(-1)
    rows = jnp.take(transfer_factors, position, axis=0)
    flows = jnp.take(line_flows, position)
    extra = jnp.zeros((position.shape[0], 128), jnp.float32).at[:, 0].set(flows)
    rows = jnp.where(valid[:, None], jnp.concatenate([rows, extra], axis=1), 0.0)
    pick = jnp.where(valid, position, 0).astype(jnp.int32)
    terminal, gathered_rows, gathered_small = exchange(
        pick, transfer_factors, ends, rows, lax.axis_size("bus"), lax.axis_size("line")
    )
    gathered_rows = gathered_rows.reshape(-1, rows.shape[1])
    gathered_small = gathered_small.reshape(-1, terminal.shape[1])
    slot_flat = slot.reshape(-1)
    outage_all = jnp.take(gathered_rows, slot_flat, axis=0)
    outage_rows = outage_all[:, :local_cols]
    outage_flows = outage_all[:, local_cols]
    outage_terms = jnp.take(gathered_small, slot_flat, axis=0)

    identity = jnp.eye(outages, dtype=jnp.float32)
    row_global = line_index * local_rows + jnp.arange(local_rows, dtype=jnp.int32)
    hit = row_global[:, None] == tripped[0][None, :]
    keep1 = 1.0 - jnp.any(hit, axis=1).astype(jnp.float32)
    hit2 = row_global[:, None] == tripped[1][None, :]
    keep12 = keep1 * (1.0 - jnp.any(hit2, axis=1).astype(jnp.float32))

    s1 = slice(0, outages)
    s2 = slice(outages, 2 * outages)
    cap1 = identity - outage_terms[s1, s1]
    rhs1 = jnp.concatenate([terminal[:, s1], outage_terms[s2, s1]], axis=0)
    w1 = solve_weights(cap1, rhs1)
    w1t_local = w1[:, :local_rows].T
    w1t_out2 = w1[:, local_rows:].T
    terminal2 = keep1[:, None] * (
        terminal[:, s2] + jnp.dot(w1t_local, outage_terms[s1, s2], precision=PRECISE)
    )
    out2 = outage_terms[s2, s2] + jnp.dot(w1t_out2, outage_terms[s1, s2], precision=PRECISE)
    cap2 = identity - out2
    w2t = solve_weights(cap2, terminal2).T
    combined = jnp.concatenate(
        [w1t_local + jnp.dot(w2t, w1t_out2, precision=PRECISE), w2t], axis=1
    )

    factors = keep12[:, None] * (
        transfer_factors + jnp.dot(combined, outage_rows, precision=PRECISE)
    )
    flows = keep12 * (line_flows + jnp.dot(combined, outage_flows, precision=PRECISE))
    return (factors, flows)


def solution(mesh):
    placed = (P("line", "bus"), P("line"), P(), P(), P())
    return jax.shard_map(
        per_device,
        mesh=mesh,
        in_specs=placed,
        out_specs=(P("line", "bus"), P("line")),
        check_vma=False,
    )
```

```python
import functools

import jax
import jax.numpy as jnp
from jax import lax
from jax.experimental import pallas as pl
from jax.experimental.pallas import tpu as pltpu
from jax.sharding import PartitionSpec as P

PRECISE = lax.Precision.HIGHEST


def _mesh_id(axis, peer):
    coords = {"line": lax.axis_index("line"), "bus": lax.axis_index("bus")}
    coords[axis] = peer
    return (coords["line"], coords["bus"])


def _greet(axis, n):
    barrier = pltpu.get_barrier_semaphore()
    me = lax.axis_index(axis)

    def body(k, carry):
        peer = lax.rem(me + k, n)
        pl.semaphore_signal(
            barrier, 1, device_id=_mesh_id(axis, peer), device_id_type=pl.DeviceIdType.MESH
        )
        return carry

    lax.fori_loop(1, n, body, 0)
    pl.semaphore_wait(barrier, n - 1)


def _remote(src, dst, send_sem, recv_sem, axis, peer):
    return pltpu.make_async_remote_copy(
        src_ref=src,
        dst_ref=dst,
        send_sem=send_sem,
        recv_sem=recv_sem,
        device_id=_mesh_id(axis, peer),
        device_id_type=pl.DeviceIdType.MESH,
    )


def _exchange_kernel(
    n_bus, n_line, pieces, pick_ref, p_ref, ends_ref, rows_ref, o_ref, o_rows, o_small,
    x_ref, recv, gathered, mine, held, picked, got, s1, r1, s2, r2, sr, rr, sl, rl,
    tsr, trr, tsl, trl,
):
    me = lax.axis_index("bus")
    here = lax.axis_index("line")
    right = lax.rem(here + 1, n_line)
    left = lax.rem(here + n_line - 1, n_line)
    chunk = x_ref.shape[0] // n_bus
    piece = rows_ref.shape[0] // pieces
    to_right = n_line // 2
    to_left = n_line - 1 - to_right
    mesh_type = pl.DeviceIdType.MESH

    barrier = pltpu.get_barrier_semaphore()

    def greet_bus(k, carry):
        pl.semaphore_signal(
            barrier, 1, device_id=_mesh_id("bus", lax.rem(me + k, n_bus)), device_id_type=mesh_type
        )
        return carry

    lax.fori_loop(1, n_bus, greet_bus, 0)
    for neighbour in (left, right):
        pl.semaphore_signal(
            barrier, 1, device_id=_mesh_id("line", neighbour), device_id_type=mesh_type
        )
    pl.semaphore_wait(barrier, n_bus - 1 + 2)

    def ring_steps(toward):
        return to_right if toward == "right" else to_left

    def ring_copy(step, part, toward, first, buf, parts, sems):
        send_right, recv_right, send_left, recv_left = sems
        if toward == "right":
            origin = lax.rem(here - (step - 1) + n_line, n_line)
            peer, send_sem, recv_sem = right, send_right, recv_right
        else:
            origin = lax.rem(here + (step - 1), n_line)
            peer, send_sem, recv_sem = left, send_left, recv_left
        size = first.shape[0] // parts
        rows = pl.ds(part * size, size)
        src = first.at[rows] if step == 1 else buf.at[origin, rows]
        slot = (step - 1) * parts + part
        return _remote(src, buf.at[origin, rows], send_sem.at[slot], recv_sem.at[slot], "line", peer)

    def big(step):
        return lambda part, toward: ring_copy(step, part, toward, rows_ref, held, pieces, (sr, rr, sl, rl))

    def small(step):
        return lambda part, toward: ring_copy(step, part, toward, picked, got, 1, (tsr, trr, tsl, trl))

    def advance(copies, step, parts):
        for part in range(parts):
            for toward in ("right", "left"):
                if step <= ring_steps(toward):
                    if step > 1:
                        copies(step - 1)(part, toward).wait_recv()
                    copies(step)(part, toward).start()

    def drain(copies, parts):
        for toward in ("right", "left"):
            last = ring_steps(toward)
            for part in range(parts):
                if last >= 1:
                    copies(last)(part, toward).wait_recv()
            for step in range(1, last + 1):
                for part in range(parts):
                    copies(step)(part, toward).wait_send()

    advance(big, 1, pieces)

    local_cols = p_ref.shape[1]
    column = lax.broadcasted_iota(jnp.int32, (local_cols, ends_ref.shape[1]), 0)
    select = (column == ends_ref[0:1, :]).astype(jnp.float32) - (
        column == ends_ref[1:2, :]
    ).astype(jnp.float32)
    x_ref[...] = jnp.dot(
        p_ref[...], select, precision=PRECISE, preferred_element_type=jnp.float32
    )

    def send1(k):
        peer = lax.rem(me + k, n_bus)
        return _remote(x_ref.at[pl.ds(peer * chunk, chunk)], recv.at[k], s1.at[k], r1.at[k], "bus", peer)

    def start1(k, carry):
        send1(k).start()
        return carry

    lax.fori_loop(1, n_bus, start1, 0)
    held[here] = rows_ref[...]
    advance(big, 2, pieces)
    total = x_ref[pl.ds(me * chunk, chunk), :]

    def finish1(k, acc):
        send1(k).wait()
        return acc + recv[k]

    total = lax.fori_loop(1, n_bus, finish1, total)
    gathered[pl.ds(me * chunk, chunk), :] = total
    mine[...] = total

    def send2(k):
        peer = lax.rem(me + k, n_bus)
        return _remote(mine, gathered.at[pl.ds(me * chunk, chunk)], s2.at[k], r2.at[k], "bus", peer)

    def start2(k, carry):
        send2(k).start()
        return carry

    lax.fori_loop(1, n_bus, start2, 0)
    advance(big, 3, pieces)

    def finish2(k, carry):
        send2(k).wait()
        return carry

    lax.fori_loop(1, n_bus, finish2, 0)

    for i in range(picked.shape[0]):
        picked[pl.ds(i, 1), :] = gathered[pl.ds(pick_ref[i], 1), :]
    got[here] = picked[...]
    advance(small, 1, 1)
    next_small = 2
    for step in range(4, to_right + 1):
        advance(big, step, pieces)
        for _ in range(1 if step == 4 else 2):
            if next_small <= to_right:
                advance(small, next_small, 1)
                next_small += 1
    for step in range(next_small, to_right + 1):
        advance(small, step, 1)
    drain(big, pieces)
    drain(small, 1)
    o_ref[...] = gathered[...]
    o_rows[...] = held[...]
    o_small[...] = got[...]


def exchange(pick, factors, ends, rows, n_bus, n_line, pieces=2):
    x = jax.ShapeDtypeStruct((factors.shape[0], ends.shape[1]), factors.dtype)
    x_rows, x_cols = x.shape
    chunk = x_rows // n_bus
    vmem = pl.BlockSpec(memory_space=pltpu.VMEM)
    smem = pl.BlockSpec(memory_space=pltpu.SMEM)
    held_shape = (n_line,) + rows.shape
    got_shape = (n_line, pick.shape[0], x_cols)
    return pl.pallas_call(
        functools.partial(_exchange_kernel, n_bus, n_line, pieces),
        out_shape=(
            jax.ShapeDtypeStruct(x.shape, x.dtype),
            jax.ShapeDtypeStruct(held_shape, rows.dtype),
            jax.ShapeDtypeStruct(got_shape, x.dtype),
        ),
        in_specs=[smem, vmem, vmem, vmem],
        out_specs=(vmem, vmem, vmem),
        scratch_shapes=[
            pltpu.VMEM(x.shape, x.dtype),
            pltpu.VMEM((n_bus, chunk, x_cols), x.dtype),
            pltpu.VMEM(x.shape, x.dtype),
            pltpu.VMEM((chunk, x_cols), x.dtype),
            pltpu.VMEM(held_shape, rows.dtype),
            pltpu.VMEM((pick.shape[0], x_cols), x.dtype),
            pltpu.VMEM(got_shape, x.dtype),
        ]
        + [pltpu.SemaphoreType.DMA((n_bus,))] * 4
        + [pltpu.SemaphoreType.DMA((n_line * pieces,))] * 4
        + [pltpu.SemaphoreType.DMA((n_line,))] * 4,
        compiler_params=pltpu.CompilerParams(
            collective_id=0, has_side_effects=True, vmem_limit_bytes=48 * 1024 * 1024
        ),
    )(pick, factors, ends, rows)


def chol_solve(factor_lower, right):
    middle = lax.linalg.triangular_solve(factor_lower, right, left_side=True, lower=True)
    return lax.linalg.triangular_solve(
        factor_lower, middle, left_side=True, lower=True, transpose_a=True
    )


def solve_weights(capacitance, terminal_rows):
    factor_lower = jnp.linalg.cholesky(jnp.dot(capacitance, capacitance.T, precision=PRECISE))
    return chol_solve(factor_lower, jnp.dot(capacitance, terminal_rows.T, precision=PRECISE))


def slot_layout(tripped, local_rows, cap):
    steps, outages = tripped.shape
    block = tripped // local_rows
    earlier = jnp.arange(outages)[None, :] < jnp.arange(outages)[:, None]
    same = (block[:, :, None] == block[:, None, :]) & earlier[None]
    rank = jnp.sum(same, axis=2).astype(jnp.int32)
    seg = jnp.arange(steps, dtype=jnp.int32)[:, None]
    slot = block * (steps * cap) + seg * cap + rank
    return block, rank, slot


def per_device(transfer_factors, line_flows, from_bus, to_bus, tripped):
    local_rows, local_cols = transfer_factors.shape
    steps, outages = tripped.shape
    cap = 8
    line_index = lax.axis_index("line")
    bus_index = lax.axis_index("bus")
    ids = tripped.reshape(-1)

    def local_column(bus):
        offset = bus - bus_index * local_cols
        return jnp.where((offset >= 0) & (offset < local_cols), offset, -1)

    ends = jnp.stack([local_column(jnp.take(from_bus, ids)), local_column(jnp.take(to_bus, ids))])

    block, rank, slot = slot_layout(tripped, local_rows, cap)
    mine = (block == line_index)[:, None, :] & (
        rank[:, None, :] == jnp.arange(cap, dtype=jnp.int32)[None, :, None]
    )
    position = jnp.sum(jnp.where(mine, (tripped - line_index * local_rows)[:, None, :], 0), axis=2)
    valid = jnp.any(mine, axis=2).reshape(-1)
    position = position.reshape(-1)
    rows = jnp.take(transfer_factors, position, axis=0)
    flows = jnp.take(line_flows, position)
    extra = jnp.zeros((position.shape[0], 128), jnp.float32).at[:, 0].set(flows)
    rows = jnp.where(valid[:, None], jnp.concatenate([rows, extra], axis=1), 0.0)
    pick = jnp.where(valid, position, 0).astype(jnp.int32)
    terminal, gathered_rows, gathered_small = exchange(
        pick, transfer_factors, ends, rows, lax.axis_size("bus"), lax.axis_size("line")
    )
    gathered_rows = gathered_rows.reshape(-1, rows.shape[1])
    gathered_small = gathered_small.reshape(-1, terminal.shape[1])
    slot_flat = slot.reshape(-1)
    outage_all = jnp.take(gathered_rows, slot_flat, axis=0)
    outage_rows = outage_all[:, :local_cols]
    outage_flows = outage_all[:, local_cols]
    outage_terms = jnp.take(gathered_small, slot_flat, axis=0)

    identity = jnp.eye(outages, dtype=jnp.float32)
    row_global = line_index * local_rows + jnp.arange(local_rows, dtype=jnp.int32)
    hit = row_global[:, None] == tripped[0][None, :]
    keep1 = 1.0 - jnp.any(hit, axis=1).astype(jnp.float32)
    hit2 = row_global[:, None] == tripped[1][None, :]
    keep12 = keep1 * (1.0 - jnp.any(hit2, axis=1).astype(jnp.float32))

    s1 = slice(0, outages)
    s2 = slice(outages, 2 * outages)
    cap1 = identity - outage_terms[s1, s1]
    rhs1 = jnp.concatenate([terminal[:, s1], outage_terms[s2, s1]], axis=0)
    w1 = solve_weights(cap1, rhs1)
    w1t_local = w1[:, :local_rows].T
    w1t_out2 = w1[:, local_rows:].T
    terminal2 = keep1[:, None] * (
        terminal[:, s2] + jnp.dot(w1t_local, outage_terms[s1, s2], precision=PRECISE)
    )
    out2 = outage_terms[s2, s2] + jnp.dot(w1t_out2, outage_terms[s1, s2], precision=PRECISE)
    cap2 = identity - out2
    w2t = solve_weights(cap2, terminal2).T
    combined = jnp.concatenate(
        [w1t_local + jnp.dot(w2t, w1t_out2, precision=PRECISE), w2t], axis=1
    )

    factors = keep12[:, None] * (
        transfer_factors + jnp.dot(combined, outage_rows, precision=PRECISE)
    )
    flows = keep12 * (line_flows + jnp.dot(combined, outage_flows, precision=PRECISE))
    return (factors, flows)


def solution(mesh):
    placed = (P("line", "bus"), P("line"), P(), P(), P())
    return jax.shard_map(
        per_device,
        mesh=mesh,
        in_specs=placed,
        out_specs=(P("line", "bus"), P("line")),
        check_vma=False,
    )
```
